256 devices in a mesh: rows: 64 (over x, z, core), sub: 4 (over y).
Axes of the slice: x: 4, y: 4, z: 8, core: 2. Of those that a mesh axis runs over, the one named last changes fastest.
Arguments:
- documents: bfloat16 [524288, 1024], P(('rows', 'sub')), may hold values from -40 to 40
- centroids: bfloat16 [1024, 1024], replicated, may hold values from -5 to 5
- cluster_mass: float32 [1024], replicated, may hold values from 0.00024414062 to 0.00390625
Outputs:
- new_centroids: bfloat16 [1024, 1024], P('sub')
- cluster_duals: float32 [1024], replicated
The draws below stay inside these ranges and needn't reach their ends.
All inputs are finite; a program needn't handle non-finite values.
Results may differ from the reference program's by a relative error of at most 0.0038.
Values may be sent and summed in bfloat16 or wider, within the bound.
No kernel may reach another device: no remote copies, remote signals or barrier semaphores. Data moves between devices by JAX's collectives and lax.ppermute only.
A program may use at most 64 MiB of HBM per device.

```python
import math
import jax
import jax.numpy as jnp
from jax import lax

D = 1024
K = 1024
ITERS = 3
NDOC = 524288


def base_centroids(key):
    inner = jax.random.fold_in(key, 11)
    values = jax.random.normal(inner, (K, D), jnp.float32)
    return jnp.clip(values, -5.0, 5.0)


def draw_centroids(key, part):
    return base_centroids(key).astype(jnp.bfloat16)


def draw_documents(key, part):
    cent = base_centroids(key)
    index = jnp.arange(NDOC)
    spread_rows = (index * 7 % 16 < 7)[:, None]
    cluster = index * K // NDOC
    noise = jax.random.normal(jax.random.fold_in(key, 23), (NDOC, D), jnp.float32)
    common = jax.random.normal(jax.random.fold_in(key, 22), (1, D), jnp.float32)
    common_weight = 0.25
    amplitude = 3.2 / math.sqrt(D)
    core = amplitude * cent[cluster] + 0.3 * noise
    diffuse = 0.4 * noise + common_weight * common
    values = jnp.where(spread_rows, diffuse, core)
    return jnp.clip(values, -40.0, 40.0).astype(jnp.bfloat16)


def setup_inputs(seed: int = 0) -> dict:
    keys = jax.random.split(jax.random.key(seed), 4)
    documents = draw_documents(jax.random.fold_in(keys[3], 71), 0)
    centroids = draw_centroids(jax.random.fold_in(keys[3], 71), 0)
    cluster_mass = jnp.clip(jnp.exp(jax.random.uniform(keys[2], (K,), jnp.float32, math.log(0.00024414062), math.log(0.00390625))), 0.00024414062, 0.00390625)
    return {"documents": documents, "centroids": centroids, "cluster_mass": cluster_mass}


TAU = 0.8
TEMP = 4.0

def reference(documents, centroids, cluster_mass):
    scores = lax.dot_general(documents, centroids, (((1,), (1,)), ((), ())), preferred_element_type=jnp.float32) * (TEMP / math.sqrt(D))
    loga = -jnp.log(jnp.asarray(NDOC, jnp.float32))
    duals = jnp.zeros((K,), jnp.float32)
    for step in range(ITERS):
        lse = jax.nn.logsumexp(scores + duals[None, :], axis=1)
        row_duals = TAU * (loga - lse)
        mass = jnp.exp(row_duals[:, None] + scores)
        column_mass = lax.optimization_barrier(jnp.sum(mass, axis=0))
        duals = TAU * (jnp.log(cluster_mass) - jnp.log(column_mass))
    plan = mass.astype(jnp.bfloat16)
    numerator = lax.dot_general(plan, documents, (((0,), (0,)), ((), ())), preferred_element_type=jnp.float32)
    new_centroids = (numerator / column_mass[:, None]).astype(jnp.bfloat16)
    return (new_centroids, duals)
```

```python
import math

import jax
import jax.numpy as jnp
from jax import lax
from jax.sharding import Mesh
from jax.sharding import PartitionSpec as P

D = 1024
ITERS = 3
TAU = 0.8
TEMP = 4.0
NX, NZ, NC, NY = 4, 8, 2, 4
AXES = ("x", "z", "c", "y")
LANES = 128


def swap_cores(value):
    return lax.ppermute(value, "c", [(0, 1), (1, 0)])


def broadcast_to_group(value, axes, size):
    return lax.all_to_all(jnp.broadcast_to(value[None], (size, *value.shape)), axes, 0, 0, tiled=True)


def sum_all(value):
    value = value + swap_cores(value)
    value = jnp.sum(broadcast_to_group(value, ("x", "y"), NX * NY), axis=0)
    return jnp.sum(broadcast_to_group(value, ("z",), NZ), axis=0)


def split_bf16(value):
    high = lax.reduce_precision(value, 8, 7)
    rest = value - high
    middle = lax.reduce_precision(rest, 8, 7)
    low = rest - middle
    return [piece.astype(jnp.bfloat16) for piece in (high, middle, low)]


def per_device(documents, centroids, cluster_mass):
    n_docs = documents.shape[0] * NX * NZ * NC * NY
    n_clusters = centroids.shape[0]
    half = documents.shape[1] // NC
    core = lax.axis_index("c")
    scores = lax.dot_general(
        documents, centroids, (((1,), (1,)), ((), ())), preferred_element_type=jnp.float32
    ) * (TEMP / math.sqrt(D))
    loga = -jnp.log(jnp.asarray(n_docs, jnp.float32))
    duals = jnp.zeros((n_clusters,), jnp.float32)
    for step in range(ITERS):
        lse = jax.nn.logsumexp(scores + duals[None, :], axis=1)
        row_duals = TAU * (loga - lse)
        mass = jnp.exp(row_duals[:, None] + scores)
        local_mass = jnp.sum(mass, axis=0).reshape(n_clusters // LANES, LANES)
        if step < ITERS - 1:
            column_mass = sum_all(local_mass).reshape(n_clusters)
            duals = TAU * (jnp.log(cluster_mass) - jnp.log(column_mass))
    plan = mass.astype(jnp.bfloat16)
    partial = lax.dot_general(
        plan, documents, (((0,), (0,)), ((), ())), preferred_element_type=jnp.float32
    )
    own = lax.dynamic_slice_in_dim(partial, core * half, half, 1)
    other = lax.dynamic_slice_in_dim(partial, (1 - core) * half, half, 1)
    local_mass = local_mass + swap_cores(local_mass)
    chip = own + swap_cores(other.astype(jnp.bfloat16)).astype(jnp.float32)
    slab = n_clusters // (NX * NY)
    pieces = [piece.reshape(1, n_clusters // half, half) for piece in split_bf16(local_mass)]
    pieces.append(jnp.zeros((1, 2, half), jnp.bfloat16))
    extra = jnp.broadcast_to(jnp.concatenate(pieces, axis=1), (NX * NY, 8, half))
    packed = jnp.concatenate([chip.astype(jnp.bfloat16).reshape(NX * NY, slab, half), extra], axis=1)
    got = lax.all_to_all(packed, ("y", "x"), 0, 0, tiled=True).astype(jnp.float32)
    slab_sum = jnp.sum(got[:, :slab], axis=0)
    mass_xy = jnp.sum(got[:, slab : slab + 2] + got[:, slab + 2 : slab + 4] + got[:, slab + 4 : slab + 6], axis=0)
    rows = slab // NZ
    packed = jnp.concatenate(
        [slab_sum.reshape(NZ, rows, half), jnp.broadcast_to(jnp.pad(mass_xy, ((0, 6), (0, 0)))[None], (NZ, 8, half))],
        axis=1,
    )
    got = lax.all_to_all(packed, ("z",), 0, 0, tiled=True)
    total = jnp.sum(got, axis=0)
    column_mass = total[rows : rows + 2].reshape(n_clusters)
    duals = TAU * (jnp.log(cluster_mass) - jnp.log(column_mass))
    first = (lax.axis_index("y") * NX + lax.axis_index("x")) * slab + lax.axis_index("z") * rows
    own_mass = lax.dynamic_slice_in_dim(column_mass, first, rows, 0)
    mine = (total[:rows] / own_mass[:, None]).astype(jnp.bfloat16)
    block = broadcast_to_group(mine, ("x", "z"), NX * NZ).reshape(n_clusters // NY, half)
    other = swap_cores(block)
    left = jnp.where(core == 0, block, other)
    right = jnp.where(core == 0, other, block)
    return jnp.concatenate([left, right], axis=1), duals


def solution(mesh):
    grid = Mesh(mesh.devices.reshape(NX, NZ, NC, NY), AXES)
    return jax.shard_map(
        per_device,
        mesh=grid,
        in_specs=(P(AXES, None), P(), P()),
        out_specs=(P("y", None), P()),
        check_vma=False,
    )
```

```python
import functools
import math

import jax
import jax.numpy as jnp
from jax import lax
from jax.experimental import pallas as pl
from jax.experimental.pallas import tpu as pltpu
from jax.sharding import Mesh
from jax.sharding import PartitionSpec as P

D = 1024
TAU = 0.8
TEMP = 4.0
NX, NZ, NC, NY = 4, 8, 2, 4
AXES = ("x", "z", "c", "y")
LANES = 128
BLOCK = 256
TILE = 256
MIB = 2**20


def swap_cores(value):
    return lax.ppermute(value, "c", [(0, 1), (1, 0)])


def broadcast_to_group(value, axes, size):
    return lax.all_to_all(jnp.broadcast_to(value[None], (size, *value.shape)), axes, 0, 0, tiled=True)


def sum_all(value):
    value = jnp.sum(broadcast_to_group(value, ("x", "y"), NX * NY), axis=0)
    return jnp.sum(broadcast_to_group(value, ("z", "c"), NZ * NC), axis=0)


def masses(scores, duals, loga):
    shifted = scores if duals is None else scores + duals
    top = jnp.max(shifted, axis=0, keepdims=True)
    lse = top + jnp.log(jnp.sum(jnp.exp(shifted - top), axis=0, keepdims=True))
    return jnp.exp(TAU * (loga - lse) + scores)


def first_kernel(loga, n_blocks, docs_ref, cent_ref, scores_ref, mass_ref, held, acc):
    step = pl.program_id(0)

    @pl.when(step == 0)
    def _():
        held[...] = jnp.zeros_like(held)
        acc[...] = jnp.zeros_like(acc)

    before = held[...]
    scores = lax.dot_general(
        cent_ref[...], docs_ref[...], (((1,), (1,)), ((), ())), preferred_element_type=jnp.float32
    ) * (TEMP / math.sqrt(D))
    total = jnp.zeros(acc.shape, jnp.float32)
    for lane in range(0, BLOCK, LANES):
        total += masses(before[:, lane : lane + LANES], None, loga)
    acc[...] += jnp.where(step > 0, total, 0.0)
    scores_ref[...] = scores
    held[...] = scores

    @pl.when(step == n_blocks)
    def _():
        mass_ref[...] = jnp.sum(acc[...].T, axis=0, keepdims=True)


def first_call(documents, centroids, loga):
    n_docs, dim = documents.shape
    n_clusters = centroids.shape[0]
    n_blocks = n_docs // BLOCK
    last = n_blocks - 1
    return pl.pallas_call(
        functools.partial(first_kernel, loga, n_blocks),
        grid=(n_blocks + 1,),
        in_specs=[
            pl.BlockSpec((BLOCK, dim), lambda i: (jnp.minimum(i, last), 0)),
            pl.BlockSpec((n_clusters, dim), lambda i: (0, 0)),
        ],
        out_specs=[
            pl.BlockSpec((n_clusters, BLOCK), lambda i: (0, jnp.minimum(i, last))),
            pl.BlockSpec((1, n_clusters), lambda i: (0, 0)),
        ],
        out_shape=[
            jax.ShapeDtypeStruct((n_clusters, n_docs), jnp.float32),
            jax.ShapeDtypeStruct((1, n_clusters), jnp.float32),
        ],
        scratch_shapes=[
            pltpu.VMEM((n_clusters, BLOCK), jnp.float32),
            pltpu.VMEM((n_clusters, LANES), jnp.float32),
        ],
        compiler_params=pltpu.CompilerParams(vmem_limit_bytes=62 * MIB),
        name="first",
    )(documents, centroids)


def start_duals(duals_ref, duals_col, acc):
    duals_col[...] = jnp.broadcast_to(duals_ref[...], (LANES, duals_ref.shape[1])).T
    acc[...] = jnp.zeros_like(acc)


def middle_kernel(loga, n_blocks, scores_ref, duals_ref, mass_ref, duals_col, acc):
    step = pl.program_id(0)

    @pl.when(step == 0)
    def _():
        start_duals(duals_ref, duals_col, acc)

    duals = duals_col[...]
    total = acc[...]
    for lane in range(0, BLOCK, LANES):
        total += masses(scores_ref[:, lane : lane + LANES], duals, loga)
    acc[...] = total

    @pl.when(step == n_blocks - 1)
    def _():
        mass_ref[...] = jnp.sum(acc[...].T, axis=0, keepdims=True)


def middle_call(scores, duals, loga):
    n_clusters, n_docs = scores.shape
    n_blocks = n_docs // BLOCK
    return pl.pallas_call(
        functools.partial(middle_kernel, loga, n_blocks),
        grid=(n_blocks,),
        in_specs=[
            pl.BlockSpec((n_clusters, BLOCK), lambda i: (0, i)),
            pl.BlockSpec((1, n_clusters), lambda i: (0, 0)),
        ],
        out_specs=pl.BlockSpec((1, n_clusters), lambda i: (0, 0)),
        out_shape=jax.ShapeDtypeStruct((1, n_clusters), jnp.float32),
        scratch_shapes=[
            pltpu.VMEM((n_clusters, LANES), jnp.float32),
            pltpu.VMEM((n_clusters, LANES), jnp.float32),
        ],
        compiler_params=pltpu.CompilerParams(vmem_limit_bytes=62 * MIB),
        name="middle",
    )(scores, duals)


def last_kernel(loga, n_blocks, n_tiles, core_ref, scores_ref, duals_ref, docs_ref, send_ref, own_ref, mass_ref, plan, duals_col, acc):
    step = pl.program_id(0)

    @pl.when(step == 0)
    def _():
        start_duals(duals_ref, duals_col, acc)

    @pl.when(step < n_blocks)
    def _():
        duals = duals_col[...]
        total = acc[...]
        for lane in range(0, BLOCK, LANES):
            mass = masses(scores_ref[:, lane : lane + LANES], duals, loga)
            total += mass
            plan[:, pl.ds(pl.multiple_of(step * BLOCK + lane, LANES), LANES)] = mass.astype(jnp.bfloat16)
        acc[...] = total

    @pl.when(step == n_blocks)
    def _():
        mass_ref[...] = jnp.sum(acc[...].T, axis=0, keepdims=True)

    def tile():
        return lax.dot_general(
            plan[...], docs_ref[...], (((1,), (0,)), ((), ())), preferred_element_type=jnp.float32
        )

    @pl.when(jnp.logical_and(step >= n_blocks, step < n_blocks + n_tiles))
    def _():
        send_ref[...] = tile().astype(jnp.bfloat16)

    @pl.when(step >= n_blocks + n_tiles)
    def _():
        own_ref[...] = tile()


def last_call(scores, duals, documents, core, loga):
    n_clusters, n_docs = scores.shape
    dim = documents.shape[1]
    half = dim // NC
    n_blocks = n_docs // BLOCK
    n_tiles = half // TILE

    def column(i, core):
        tile = jnp.clip(i - n_blocks, 0, 2 * n_tiles - 1)
        return lax.rem(tile + (1 - core[0]) * n_tiles, 2 * n_tiles)

    return pl.pallas_call(
        functools.partial(last_kernel, loga, n_blocks, n_tiles),
        grid_spec=pltpu.PrefetchScalarGridSpec(
            num_scalar_prefetch=1,
            grid=(n_blocks + 2 * n_tiles,),
            in_specs=[
                pl.BlockSpec((n_clusters, BLOCK), lambda i, core: (0, jnp.minimum(i, n_blocks - 1))),
                pl.BlockSpec((1, n_clusters), lambda i, core: (0, 0)),
                pl.BlockSpec((n_docs, TILE), lambda i, core: (0, column(i, core))),
            ],
            out_specs=[
                pl.BlockSpec((n_clusters, TILE), lambda i, core: (0, jnp.clip(i - n_blocks, 0, n_tiles - 1))),
                pl.BlockSpec((n_clusters, TILE), lambda i, core: (0, jnp.clip(i - n_blocks - n_tiles, 0, n_tiles - 1))),
                pl.BlockSpec((1, n_clusters), lambda i, core: (0, 0)),
            ],
            scratch_shapes=[
                pltpu.VMEM((n_clusters, n_docs), jnp.bfloat16),
                pltpu.VMEM((n_clusters, LANES), jnp.float32),
                pltpu.VMEM((n_clusters, LANES), jnp.float32),
            ],
        ),
        out_shape=[
            pltpu.VMEM((n_clusters, half), jnp.bfloat16),
            pltpu.VMEM((n_clusters, half), jnp.float32),
            pltpu.VMEM((1, n_clusters), jnp.float32),
        ],
        compiler_params=pltpu.CompilerParams(vmem_limit_bytes=56 * MIB),
        name="last",
    )(core, scores, duals, documents)


def pack_kernel(per_step, slab, own_ref, got_ref, mass_ref, mass_got_ref, out_ref):
    half = own_ref.shape[1]
    total = own_ref[...] + got_ref[...].astype(jnp.float32)
    out_ref[:, :slab, :] = total.astype(jnp.bfloat16).reshape(per_step, slab, half)
    mass = mass_ref[...] + mass_got_ref[...]
    high = mass.astype(jnp.bfloat16).astype(jnp.float32)
    middle = (mass - high).astype(jnp.bfloat16).astype(jnp.float32)
    low = mass - high - middle
    rows = lax.broadcasted_iota(jnp.int32, (8, half), 0)
    extra = jnp.zeros((8, half), jnp.float32)
    for index, piece in enumerate((high, middle, low)):
        for part in range(2):
            row = jnp.broadcast_to(piece[:, part * half : (part + 1) * half], (8, half))
            extra = jnp.where(rows == 2 * index + part, row, extra)
    extra = extra.astype(jnp.bfloat16)
    for k in range(per_step):
        out_ref[k, slab:, :] = extra


def pack_call(own, got, mass, mass_got):
    n_clusters, half = own.shape
    slab = n_clusters // (NX * NY)
    per_step = 4
    steps = NX * NY // per_step
    return pl.pallas_call(
        functools.partial(pack_kernel, per_step, slab),
        grid=(steps,),
        in_specs=[
            pl.BlockSpec((per_step * slab, half), lambda i: (i, 0)),
            pl.BlockSpec((per_step * slab, half), lambda i: (i, 0)),
            pl.BlockSpec((1, n_clusters), lambda i: (0, 0)),
            pl.BlockSpec((1, n_clusters), lambda i: (0, 0)),
        ],
        out_specs=pl.BlockSpec((per_step, slab + 8, half), lambda i: (i, 0, 0)),
        out_shape=jax.ShapeDtypeStruct((NX * NY, slab + 8, half), jnp.bfloat16),
        compiler_params=pltpu.CompilerParams(vmem_limit_bytes=16 * MIB),
        name="pack",
    )(own, got, mass, mass_got)


def repack_kernel(slab, got_ref, out_ref):
    n_slabs, rows = got_ref.shape[0], slab // NZ
    total = got_ref[0].astype(jnp.float32)
    for k in range(1, n_slabs):
        total += got_ref[k].astype(jnp.float32)
    out_ref[:, :rows, :] = total[:slab].reshape(NZ, rows, total.shape[1])
    extra = total[slab:]
    extra = extra + pltpu.roll(extra, 6, 0) + pltpu.roll(extra, 4, 0)
    for k in range(NZ):
        out_ref[k, rows:, :] = extra


def repack_call(got, slab):
    half = got.shape[2]
    return pl.pallas_call(
        functools.partial(repack_kernel, slab),
        in_specs=[pl.BlockSpec(memory_space=pltpu.VMEM)],
        out_specs=pl.BlockSpec(memory_space=pltpu.VMEM),
        out_shape=jax.ShapeDtypeStruct((NZ, slab // NZ + 8, half), jnp.float32),
        compiler_params=pltpu.CompilerParams(vmem_limit_bytes=16 * MIB),
        name="repack",
    )(got)


def finish_kernel(rows, place_ref, got_ref, out_ref, mass_ref):
    total = got_ref[0]
    for k in range(1, got_ref.shape[0]):
        total += got_ref[k]
    half = total.shape[1]
    place = place_ref[0]
    mass = total[rows:]
    mass_ref[...] = mass
    part = place // half
    row = jnp.where(part == 0, mass[0:1], mass[1:2])
    lane = lax.broadcasted_iota(jnp.int32, (rows, half), 1)
    first = place - part * half
    mine = lane == first + lax.broadcasted_iota(jnp.int32, (rows, half), 0)
    own_mass = jnp.sum(jnp.where(mine, jnp.broadcast_to(row, (rows, half)), 0.0), axis=1, keepdims=True)
    centroids = (total[:rows] / own_mass).astype(jnp.bfloat16)
    for k in range(out_ref.shape[0]):
        out_ref[k] = centroids


def finish_call(got, place, rows):
    half = got.shape[2]
    return pl.pallas_call(
        functools.partial(finish_kernel, rows),
        grid_spec=pltpu.PrefetchScalarGridSpec(
            num_scalar_prefetch=1,
            grid=(1,),
            in_specs=[pl.BlockSpec(got.shape, lambda i, place: (0, 0, 0))],
            out_specs=[
                pl.BlockSpec((NX * NZ, rows, half), lambda i, place: (0, 0, 0)),
                pl.BlockSpec((8, half), lambda i, place: (0, 0)),
            ],
        ),
        out_shape=[
            jax.ShapeDtypeStruct((NX * NZ, rows, half), jnp.bfloat16),
            jax.ShapeDtypeStruct((8, half), jnp.float32),
        ],
        compiler_params=pltpu.CompilerParams(vmem_limit_bytes=16 * MIB),
        name="finish",
    )(place, got)


def join_kernel(core_ref, block_ref, other_ref, out_ref):
    half = block_ref.shape[1]
    core = core_ref[0]
    out_ref[:, pl.ds(pl.multiple_of(core * half, half), half)] = block_ref[...]
    out_ref[:, pl.ds(pl.multiple_of((1 - core) * half, half), half)] = other_ref[...]


def join_call(core, block, other):
    rows, half = block.shape
    return pl.pallas_call(
        join_kernel,
        grid_spec=pltpu.PrefetchScalarGridSpec(
            num_scalar_prefetch=1,
            grid=(1,),
            in_specs=[pl.BlockSpec((rows, half), lambda i, core: (0, 0))] * 2,
            out_specs=pl.BlockSpec((rows, 2 * half), lambda i, core: (0, 0)),
        ),
        out_shape=jax.ShapeDtypeStruct((rows, 2 * half), jnp.bfloat16),
        compiler_params=pltpu.CompilerParams(vmem_limit_bytes=16 * MIB),
        name="join",
    )(core, block, other)


def per_device(documents, centroids, cluster_mass):
    n_docs = documents.shape[0] * NX * NZ * NC * NY
    n_clusters = centroids.shape[0]
    half = documents.shape[1] // NC
    core = lax.axis_index("c")
    slab = n_clusters // (NX * NY)
    rows = slab // NZ
    place = (lax.axis_index("y") * NX + lax.axis_index("x")) * slab + lax.axis_index("z") * rows
    loga = -math.log(n_docs)
    documents, core, place = lax.optimization_barrier((documents, core.reshape(1), place.reshape(1)))

    def duals_of(column_mass):
        return TAU * (jnp.log(cluster_mass) - jnp.log(column_mass.reshape(n_clusters)))

    def everywhere(mass):
        return sum_all(mass.reshape(n_clusters // LANES, LANES))

    scores, mass = first_call(documents, centroids, loga)
    duals = duals_of(everywhere(mass)).reshape(1, n_clusters)
    mass = middle_call(scores, duals, loga)
    duals = duals_of(everywhere(mass)).reshape(1, n_clusters)
    send, own, mass = last_call(scores, duals, documents, core, loga)
    packed = pack_call(own, swap_cores(send), mass, swap_cores(mass))
    packed = repack_call(lax.all_to_all(packed, ("y", "x"), 0, 0, tiled=True), slab)
    packed = lax.all_to_all(packed, ("z",), 0, 0, tiled=True)
    mine, column_mass = finish_call(packed, place, rows)
    block = lax.all_to_all(mine, ("x", "z"), 0, 0, tiled=True).reshape(n_clusters // NY, half)
    return join_call(core, block, swap_cores(block)), duals_of(column_mass[:2])


def solution(mesh):
    grid = Mesh(mesh.devices.reshape(NX, NZ, NC, NY), AXES)
    return jax.shard_map(
        per_device,
        mesh=grid,
        in_specs=(P(AXES, None), P(), P()),
        out_specs=(P("y", None), P()),
        check_vma=False,
    )
```

```python
import functools
import math

import jax
import jax.numpy as jnp
from jax import lax
from jax.experimental import pallas as pl
from jax.experimental.pallas import tpu as pltpu
from jax.sharding import Mesh
from jax.sharding import PartitionSpec as P

D = 1024
TAU = 0.8
TEMP = 4.0
NX, NZ, NC, NY = 4, 8, 2, 4
AXES = ("x", "z", "c", "y")
LANES = 128
BLOCK = 512
CHUNK = 64
LOG2E = 1 / math.log(2)
TILE = 256
MIB = 2**20


def swap_cores(value):
    return lax.ppermute(value, "c", [(0, 1), (1, 0)])


def fold(value, op):
    return op(value.reshape(value.shape[0] // 8, 8, value.shape[1]), axis=0)


def block_masses(scores_ref, columns, duals_ref, loga, emit):
    n_clusters = scores_ref.shape[0]
    width = columns.stop - columns.start

    def shifted(row):
        value = scores_ref[row : row + CHUNK, columns]
        if duals_ref is None:
            return value
        duals = duals_ref[row : row + CHUNK, :]
        return value + jnp.concatenate([duals] * (width // LANES), axis=1)

    top = fold(shifted(0), jnp.max)
    for row in range(CHUNK, n_clusters, CHUNK):
        top = jnp.maximum(top, fold(shifted(row), jnp.max))
    top = jnp.max(top, axis=0, keepdims=True)
    total = fold(jnp.exp2(shifted(0) - top), jnp.sum)
    for row in range(CHUNK, n_clusters, CHUNK):
        total += fold(jnp.exp2(shifted(row) - top), jnp.sum)
    lse = top + jnp.log2(jnp.sum(total, axis=0, keepdims=True))
    row_duals = TAU * (loga - lse)
    for row in range(0, n_clusters, CHUNK):
        emit(row, jnp.exp2(scores_ref[row : row + CHUNK, columns] + row_duals))


def add_lanes(acc, row, mass):
    total = mass[:, :LANES]
    for lane in range(LANES, mass.shape[1], LANES):
        total += mass[:, lane : lane + LANES]
    acc[row : row + CHUNK, :] += total


def column_sums(acc, out_ref):
    rows = [jnp.sum(acc[k : k + LANES, :].T, axis=0, keepdims=True) for k in range(0, acc.shape[0], LANES)]
    sums = jnp.concatenate(rows, axis=0)
    for slot in range(out_ref.shape[0]):
        out_ref[slot] = sums


def start_duals(got_ref, cluster_mass_ref, duals_col):
    column_mass = got_ref[0]
    for slot in range(1, got_ref.shape[0]):
        column_mass += got_ref[slot]
    duals = TAU * (jnp.log2(cluster_mass_ref[...]) - jnp.log2(column_mass))
    for k in range(duals.shape[0]):
        row = jnp.broadcast_to(duals[k : k + 1, :], (LANES, LANES))
        duals_col[k * LANES : (k + 1) * LANES, :] = row.T


def first_kernel(loga, docs_hbm, cent_hbm, scores_ref, mass_ref, docs_ref, cent_ref, acc, sems):
    n_blocks = scores_ref.shape[0]
    copies = [pltpu.make_async_copy(cent_hbm, cent_ref, sems.at[n_blocks])]
    for block in range(n_blocks):
        rows = pl.ds(block * BLOCK, BLOCK)
        copies.append(pltpu.make_async_copy(docs_hbm.at[rows], docs_ref.at[rows], sems.at[block]))
    for copy in copies:
        copy.start()
    acc[...] = jnp.zeros_like(acc)
    copies[0].wait()
    for block in range(n_blocks + 1):
        if block < n_blocks:
            copies[block + 1].wait()
            scores_ref[block] = lax.dot_general(
                cent_ref[...],
                docs_ref[block * BLOCK : (block + 1) * BLOCK, :],
                (((1,), (1,)), ((), ())),
                preferred_element_type=jnp.float32,
            ) * (TEMP / math.sqrt(D) * LOG2E)
        if block > 0:
            block_masses(scores_ref.at[block - 1], slice(0, BLOCK), None, loga, functools.partial(add_lanes, acc))
    column_sums(acc, mass_ref)


def first_call(documents, centroids, loga):
    n_docs, dim = documents.shape
    n_clusters = centroids.shape[0]
    n_blocks = n_docs // BLOCK
    vmem = pl.BlockSpec(memory_space=pltpu.VMEM)
    return pl.pallas_call(
        functools.partial(first_kernel, loga),
        in_specs=[pl.BlockSpec(memory_space=pltpu.HBM)] * 2,
        out_specs=[vmem] * 3,
        out_shape=[
            pltpu.VMEM((n_blocks, n_clusters, BLOCK), jnp.float32),
            pltpu.VMEM((NX * NY, n_clusters // LANES, LANES), jnp.float32),
            pltpu.VMEM((n_docs, dim), jnp.bfloat16),
        ],
        scratch_shapes=[
            pltpu.VMEM((n_clusters, dim), jnp.bfloat16),
            pltpu.VMEM((n_clusters, LANES), jnp.float32),
            pltpu.SemaphoreType.DMA((n_blocks + 1,)),
        ],
        compiler_params=pltpu.CompilerParams(vmem_limit_bytes=50 * MIB),
        name="first",
    )(documents, centroids)


def middle_kernel(loga, scores_ref, got_ref, cluster_mass_ref, mass_ref, duals_col, acc):
    start_duals(got_ref, cluster_mass_ref, duals_col)
    acc[...] = jnp.zeros_like(acc)

    @pl.loop(0, scores_ref.shape[0])
    def _(block):
        block_masses(scores_ref.at[block], slice(0, BLOCK), duals_col, loga, functools.partial(add_lanes, acc))

    column_sums(acc, mass_ref)


def middle_call(scores, got, cluster_mass, loga):
    n_clusters = scores.shape[1]
    vmem = pl.BlockSpec(memory_space=pltpu.VMEM)
    return pl.pallas_call(
        functools.partial(middle_kernel, loga),
        in_specs=[vmem] * 3,
        out_specs=vmem,
        out_shape=pltpu.VMEM((NX * NY, n_clusters // LANES, LANES), jnp.float32),
        scratch_shapes=[
            pltpu.VMEM((n_clusters, LANES), jnp.float32),
            pltpu.VMEM((n_clusters, LANES), jnp.float32),
        ],
        compiler_params=pltpu.CompilerParams(vmem_limit_bytes=8 * MIB),
        name="middle",
    )(scores, got, cluster_mass)


def last_kernel(loga, core_ref, scores_ref, got_ref, cluster_mass_ref, docs_ref, send_ref, own_ref, mass_ref, plan, duals_col, acc):
    start_duals(got_ref, cluster_mass_ref, duals_col)
    acc[...] = jnp.zeros_like(acc)

    @pl.loop(0, scores_ref.shape[0])
    def _(block):
        def emit(row, mass):
            add_lanes(acc, row, mass)
            columns = pl.ds(pl.multiple_of(block * BLOCK, BLOCK), BLOCK)
            plan[row : row + CHUNK, columns] = mass.astype(jnp.bfloat16)

        block_masses(scores_ref.at[block], slice(0, BLOCK), duals_col, loga, emit)

    column_sums(acc, mass_ref)
    half = own_ref.shape[1]
    for out_ref, owner in ((send_ref, 1 - core_ref[0]), (own_ref, core_ref[0])):
        for tile in range(0, half, TILE):
            columns = pl.ds(pl.multiple_of(owner * half + tile, TILE), TILE)
            out_ref[:, tile : tile + TILE] = lax.dot_general(
                plan[...], docs_ref[:, columns], (((1,), (0,)), ((), ())), preferred_element_type=jnp.float32
            ).astype(out_ref.dtype)


def last_call(scores, got, cluster_mass, documents, core, loga):
    n_clusters = scores.shape[1]
    n_docs, dim = documents.shape
    half = dim // NC
    vmem = pl.BlockSpec(memory_space=pltpu.VMEM)
    return pl.pallas_call(
        functools.partial(last_kernel, loga),
        in_specs=[pl.BlockSpec(memory_space=pltpu.SMEM)] + [vmem] * 4,
        out_specs=[vmem] * 3,
        out_shape=[
            pltpu.VMEM((n_clusters, half), jnp.bfloat16),
            pltpu.VMEM((n_clusters, half), jnp.float32),
            pltpu.VMEM((1, n_clusters // LANES, LANES), jnp.float32),
        ],
        scratch_shapes=[
            pltpu.VMEM((n_clusters, n_docs), jnp.bfloat16),
            pltpu.VMEM((n_clusters, LANES), jnp.float32),
            pltpu.VMEM((n_clusters, LANES), jnp.float32),
        ],
        compiler_params=pltpu.CompilerParams(vmem_limit_bytes=20 * MIB),
        name="last",
    )(core, scores, got, cluster_mass, documents)


def sum_kernel(got_ref, out_ref):
    total = got_ref[0]
    for slot in range(1, got_ref.shape[0]):
        total += got_ref[slot]
    for slot in range(out_ref.shape[0]):
        out_ref[slot] = total


def sum_call(got, copies):
    vmem = pl.BlockSpec(memory_space=pltpu.VMEM)
    return pl.pallas_call(
        sum_kernel,
        in_specs=[vmem],
        out_specs=vmem,
        out_shape=pltpu.VMEM((copies, *got.shape[1:]), got.dtype),
        compiler_params=pltpu.CompilerParams(vmem_limit_bytes=4 * MIB),
        name="sum",
    )(got)


def pack_kernel(own_ref, got_ref, mass_ref, mass_got_ref, out_ref):
    half = own_ref.shape[1]
    n_slabs = out_ref.shape[0]
    slab = own_ref.shape[0] // n_slabs
    mass = mass_ref[0] + mass_got_ref[0]
    high = mass.astype(jnp.bfloat16)
    middle = (mass - high.astype(jnp.float32)).astype(jnp.bfloat16)
    low = (mass - high.astype(jnp.float32) - middle.astype(jnp.float32)).astype(jnp.bfloat16)
    rest = jnp.zeros((mass.shape[0], half - 3 * LANES), jnp.bfloat16)
    extra = jnp.concatenate([high, middle, low, rest], axis=1)
    for k in range(n_slabs):
        rows = slice(k * slab, (k + 1) * slab)
        out_ref[k, :slab, :] = (own_ref[rows, :] + got_ref[rows, :].astype(jnp.float32)).astype(jnp.bfloat16)
        out_ref[k, slab:, :] = extra


def pack_call(own, got, mass, mass_got):
    n_clusters, half = own.shape
    n_slabs = NX * NY
    vmem = pl.BlockSpec(memory_space=pltpu.VMEM)
    return pl.pallas_call(
        pack_kernel,
        in_specs=[vmem] * 4,
        out_specs=vmem,
        out_shape=pltpu.VMEM((n_slabs, n_clusters // n_slabs + mass.shape[1], half), jnp.bfloat16),
        compiler_params=pltpu.CompilerParams(vmem_limit_bytes=8 * MIB),
        name="pack",
    )(own, got, mass, mass_got)


def repack_kernel(slab, got_ref, out_ref):
    rows = slab // NZ
    total = got_ref[0].astype(jnp.float32)
    for k in range(1, got_ref.shape[0]):
        total += got_ref[k].astype(jnp.float32)
    extra = total[slab:]
    extra = extra + jnp.concatenate([extra[:, LANES:], extra[:, :LANES]], axis=1) + jnp.concatenate(
        [extra[:, 2 * LANES :], extra[:, : 2 * LANES]], axis=1
    )
    for k in range(NZ):
        out_ref[k, :rows, :] = total[k * rows : (k + 1) * rows]
        out_ref[k, rows:, :] = extra


def repack_call(got, slab):
    vmem = pl.BlockSpec(memory_space=pltpu.VMEM)
    shape = (NZ, slab // NZ + got.shape[1] - slab, got.shape[2])
    return pl.pallas_call(
        functools.partial(repack_kernel, slab),
        in_specs=[vmem],
        out_specs=vmem,
        out_shape=pltpu.VMEM(shape, jnp.float32),
        compiler_params=pltpu.CompilerParams(vmem_limit_bytes=8 * MIB),
        name="repack",
    )(got)


def finish_kernel(rows, place_ref, got_ref, cluster_mass_ref, out_ref, duals_ref):
    total = got_ref[0]
    for k in range(1, got_ref.shape[0]):
        total += got_ref[k]
    mass = total[rows:, :LANES]
    duals_ref[...] = TAU * (jnp.log(cluster_mass_ref[...]) - jnp.log(mass))
    place = place_ref[0]
    group = place // LANES
    first = place - group * LANES
    row = lax.broadcasted_iota(jnp.int32, mass.shape, 0)
    lane = lax.broadcasted_iota(jnp.int32, mass.shape, 1)
    line = jnp.sum(jnp.where(row == group, mass, 0.0), axis=0, keepdims=True)
    mine = jnp.where(lane == row + first, jnp.broadcast_to(line, mass.shape), 0.0)
    own_mass = jnp.sum(mine, axis=1, keepdims=True)
    centroids = (total[:rows] / own_mass).astype(jnp.bfloat16)
    for k in range(out_ref.shape[0]):
        out_ref[k] = centroids


def finish_call(got, cluster_mass, place, rows):
    half = got.shape[2]
    vmem = pl.BlockSpec(memory_space=pltpu.VMEM)
    return pl.pallas_call(
        functools.partial(finish_kernel, rows),
        in_specs=[pl.BlockSpec(memory_space=pltpu.SMEM), vmem, vmem],
        out_specs=[vmem, vmem],
        out_shape=[
            pltpu.VMEM((NX * NZ, rows, half), jnp.bfloat16),
            jax.ShapeDtypeStruct(cluster_mass.shape, jnp.float32),
        ],
        compiler_params=pltpu.CompilerParams(vmem_limit_bytes=8 * MIB),
        name="finish",
    )(place, got, cluster_mass)


def join_kernel(core_ref, block_ref, other_ref, out_ref):
    half = block_ref.shape[1]
    core = core_ref[0]
    out_ref[:, pl.ds(pl.multiple_of(core * half, half), half)] = block_ref[...]
    out_ref[:, pl.ds(pl.multiple_of((1 - core) * half, half), half)] = other_ref[...]


def join_call(core, block, other):
    rows, half = block.shape
    vmem = pl.BlockSpec(memory_space=pltpu.VMEM)
    return pl.pallas_call(
        join_kernel,
        in_specs=[pl.BlockSpec(memory_space=pltpu.SMEM), vmem, vmem],
        out_specs=vmem,
        out_shape=jax.ShapeDtypeStruct((rows, 2 * half), jnp.bfloat16),
        compiler_params=pltpu.CompilerParams(vmem_limit_bytes=8 * MIB),
        name="join",
    )(core, block, other)


def sum_all(copies):
    got = lax.all_to_all(copies, ("x", "y"), 0, 0, tiled=True)
    return lax.all_to_all(sum_call(got, NZ * NC), ("z", "c"), 0, 0, tiled=True)


def per_device(documents, centroids, cluster_mass):
    n_docs = documents.shape[0] * NX * NZ * NC * NY
    n_clusters = centroids.shape[0]
    half = documents.shape[1] // NC
    core = lax.axis_index("c")
    slab = n_clusters // (NX * NY)
    rows = slab // NZ
    place = (lax.axis_index("y") * NX + lax.axis_index("x")) * slab + lax.axis_index("z") * rows
    documents, core, place = lax.optimization_barrier((documents, core.reshape(1), place.reshape(1)))
    loga = -math.log2(n_docs)
    cluster_mass = cluster_mass.reshape(n_clusters // LANES, LANES)
    scores, mass, documents = first_call(documents, centroids, loga)
    mass = middle_call(scores, sum_all(mass), cluster_mass, loga)
    send, own, mass = last_call(scores, sum_all(mass), cluster_mass, documents, core, loga)
    packed = pack_call(own, swap_cores(send), mass, swap_cores(mass))
    packed = repack_call(lax.all_to_all(packed, ("y", "x"), 0, 0, tiled=True), slab)
    packed = lax.all_to_all(packed, ("z",), 0, 0, tiled=True)
    mine, duals = finish_call(packed, cluster_mass, place, rows)
    block = lax.all_to_all(mine, ("x", "z"), 0, 0, tiled=True).reshape(n_clusters // NY, half)
    return join_call(core, block, swap_cores(block)), duals.reshape(n_clusters)


def solution(mesh):
    grid = Mesh(mesh.devices.reshape(NX, NZ, NC, NY), AXES)
    return jax.shard_map(
        per_device,
        mesh=grid,
        in_specs=(P(AXES, None), P(), P()),
        out_specs=(P("y", None), P()),
        check_vma=False,
    )
```

```python
import functools
import math

import jax
import jax.numpy as jnp
from jax import lax
from jax.experimental import pallas as pl
from jax.experimental.pallas import tpu as pltpu
from jax.sharding import Mesh
from jax.sharding import PartitionSpec as P

D = 1024
TAU = 0.8
TEMP = 4.0
NX, NZ, NC, NY = 4, 8, 2, 4
AXES = ("x", "z", "c", "y")
LANES = 128
BLOCK = 512
CHUNK = 64
LOG2E = 1 / math.log(2)
MIB = 2**20


def swap_cores(value):
    return lax.ppermute(value, "c", [(0, 1), (1, 0)])


def fold(value, op):
    return op(value.reshape(value.shape[0] // 8, 8, value.shape[1]), axis=0)


def block_masses(scores_ref, columns, duals_ref, loga, emit):
    n_clusters = scores_ref.shape[0]
    width = columns.stop - columns.start

    def shifted(row):
        value = scores_ref[row : row + CHUNK, columns]
        if duals_ref is None:
            return value
        duals = duals_ref[row : row + CHUNK, :]
        return value + jnp.concatenate([duals] * (width // LANES), axis=1)

    top = fold(shifted(0), jnp.max)
    for row in range(CHUNK, n_clusters, CHUNK):
        top = jnp.maximum(top, fold(shifted(row), jnp.max))
    top = jnp.max(top, axis=0, keepdims=True)
    total = fold(jnp.exp2(shifted(0) - top), jnp.sum)
    for row in range(CHUNK, n_clusters, CHUNK):
        total += fold(jnp.exp2(shifted(row) - top), jnp.sum)
    lse = top + jnp.log2(jnp.sum(total, axis=0, keepdims=True))
    row_duals = TAU * (loga - lse)
    for row in range(0, n_clusters, CHUNK):
        emit(row, jnp.exp2(scores_ref[row : row + CHUNK, columns] + row_duals))


def add_lanes(acc, row, mass):
    total = mass[:, :LANES]
    for lane in range(LANES, mass.shape[1], LANES):
        total += mass[:, lane : lane + LANES]
    acc[row : row + CHUNK, :] += total


def column_sums(acc, out_ref):
    rows = [jnp.sum(acc[k : k + LANES, :].T, axis=0, keepdims=True) for k in range(0, acc.shape[0], LANES)]
    sums = jnp.concatenate(rows, axis=0)
    for slot in range(out_ref.shape[0]):
        out_ref[slot] = sums


def start_duals(got_ref, cluster_mass_ref, duals_col):
    column_mass = got_ref[0]
    for slot in range(1, got_ref.shape[0]):
        column_mass += got_ref[slot]
    duals = TAU * (jnp.log2(cluster_mass_ref[...]) - jnp.log2(column_mass))
    for k in range(duals.shape[0]):
        row = jnp.broadcast_to(duals[k : k + 1, :], (LANES, LANES))
        duals_col[k * LANES : (k + 1) * LANES, :] = row.T


def first_kernel(loga, docs_hbm, cent_hbm, scores_ref, mass_ref, docs_ref, cent_ref, acc, sems):
    n_blocks = scores_ref.shape[0]
    copies = [pltpu.make_async_copy(cent_hbm, cent_ref, sems.at[n_blocks])]
    for block in range(n_blocks):
        rows = pl.ds(block * BLOCK, BLOCK)
        copies.append(pltpu.make_async_copy(docs_hbm.at[rows], docs_ref.at[rows], sems.at[block]))
    copies[0].start()
    copies[1].start()
    acc[...] = jnp.zeros_like(acc)
    copies[0].wait()
    for block in range(n_blocks + 1):
        if block < n_blocks:
            copies[block + 1].wait()
            if block == 0:
                for copy in copies[2:]:
                    copy.start()
            scores_ref[block] = lax.dot_general(
                cent_ref[...],
                docs_ref[block * BLOCK : (block + 1) * BLOCK, :],
                (((1,), (1,)), ((), ())),
                preferred_element_type=jnp.float32,
            ) * (TEMP / math.sqrt(D) * LOG2E)
        if block > 0:
            block_masses(scores_ref.at[block - 1], slice(0, BLOCK), None, loga, functools.partial(add_lanes, acc))
    column_sums(acc, mass_ref)


def first_call(documents, centroids, loga):
    n_docs, dim = documents.shape
    n_clusters = centroids.shape[0]
    n_blocks = n_docs // BLOCK
    vmem = pl.BlockSpec(memory_space=pltpu.VMEM)
    return pl.pallas_call(
        functools.partial(first_kernel, loga),
        in_specs=[pl.BlockSpec(memory_space=pltpu.HBM)] * 2,
        out_specs=[vmem] * 3,
        out_shape=[
            pltpu.VMEM((n_blocks, n_clusters, BLOCK), jnp.float32),
            pltpu.VMEM((NX * NY, n_clusters // LANES, LANES), jnp.float32),
            pltpu.VMEM((n_docs, dim), jnp.bfloat16),
        ],
        scratch_shapes=[
            pltpu.VMEM((n_clusters, dim), jnp.bfloat16),
            pltpu.VMEM((n_clusters, LANES), jnp.float32),
            pltpu.SemaphoreType.DMA((n_blocks + 1,)),
        ],
        compiler_params=pltpu.CompilerParams(vmem_limit_bytes=50 * MIB),
        name="first",
    )(documents, centroids)


def middle_kernel(loga, scores_ref, got_ref, cluster_mass_ref, mass_ref, duals_col, acc):
    start_duals(got_ref, cluster_mass_ref, duals_col)
    acc[...] = jnp.zeros_like(acc)

    @pl.loop(0, scores_ref.shape[0])
    def _(block):
        block_masses(scores_ref.at[block], slice(0, BLOCK), duals_col, loga, functools.partial(add_lanes, acc))

    column_sums(acc, mass_ref)


def middle_call(scores, got, cluster_mass, loga):
    n_clusters = scores.shape[1]
    vmem = pl.BlockSpec(memory_space=pltpu.VMEM)
    return pl.pallas_call(
        functools.partial(middle_kernel, loga),
        in_specs=[vmem] * 3,
        out_specs=vmem,
        out_shape=pltpu.VMEM((NX * NY, n_clusters // LANES, LANES), jnp.float32),
        scratch_shapes=[
            pltpu.VMEM((n_clusters, LANES), jnp.float32),
            pltpu.VMEM((n_clusters, LANES), jnp.float32),
        ],
        compiler_params=pltpu.CompilerParams(vmem_limit_bytes=8 * MIB),
        name="middle",
    )(scores, got, cluster_mass)


def half_columns(core, half):
    return pl.ds(pl.multiple_of(core * half, half), half)


def last_kernel(loga, core_ref, scores_ref, got_ref, cluster_mass_ref, docs_ref, send_ref, plan_ref, mass_ref, total, duals_col, acc):
    n_blocks = scores_ref.shape[0]
    columns = half_columns(1 - core_ref[0], send_ref.shape[1])
    start_duals(got_ref, cluster_mass_ref, duals_col)
    acc[...] = jnp.zeros_like(acc)
    for block in range(n_blocks + 1):
        if block > 0:
            rows = slice((block - 1) * BLOCK, block * BLOCK)
            part = lax.dot_general(
                plan_ref[:, rows], docs_ref[rows, columns], (((1,), (0,)), ((), ())), preferred_element_type=jnp.float32
            )
            if block > 1:
                part += total[...]
            if block < n_blocks:
                total[...] = part
            else:
                send_ref[...] = part.astype(jnp.bfloat16)
        if block < n_blocks:

            def emit(row, mass, start=block * BLOCK):
                add_lanes(acc, row, mass)
                plan_ref[row : row + CHUNK, start : start + BLOCK] = mass.astype(jnp.bfloat16)

            block_masses(scores_ref.at[block], slice(0, BLOCK), duals_col, loga, emit)
    column_sums(acc, mass_ref)


def last_call(scores, got, cluster_mass, documents, core, loga):
    n_clusters = scores.shape[1]
    n_docs, dim = documents.shape
    half = dim // NC
    vmem = pl.BlockSpec(memory_space=pltpu.VMEM)
    return pl.pallas_call(
        functools.partial(last_kernel, loga),
        in_specs=[pl.BlockSpec(memory_space=pltpu.SMEM)] + [vmem] * 4,
        out_specs=[vmem] * 3,
        out_shape=[
            pltpu.VMEM((n_clusters, half), jnp.bfloat16),
            pltpu.VMEM((n_clusters, n_docs), jnp.bfloat16),
            pltpu.VMEM((1, n_clusters // LANES, LANES), jnp.float32),
        ],
        scratch_shapes=[
            pltpu.VMEM((n_clusters, half), jnp.float32),
            pltpu.VMEM((n_clusters, LANES), jnp.float32),
            pltpu.VMEM((n_clusters, LANES), jnp.float32),
        ],
        compiler_params=pltpu.CompilerParams(vmem_limit_bytes=16 * MIB),
        name="last",
    )(core, scores, got, cluster_mass, documents)


def own_kernel(core_ref, plan_ref, docs_ref, own_ref):
    half = own_ref.shape[1]
    own_ref[...] = lax.dot_general(
        plan_ref[...],
        docs_ref[:, half_columns(core_ref[0], half)],
        (((1,), (0,)), ((), ())),
        preferred_element_type=jnp.float32,
    )


def own_call(plan, documents, core):
    n_clusters, n_docs = plan.shape
    half = documents.shape[1] // NC
    vmem = pl.BlockSpec(memory_space=pltpu.VMEM)
    return pl.pallas_call(
        own_kernel,
        in_specs=[pl.BlockSpec(memory_space=pltpu.SMEM), vmem, vmem],
        out_specs=vmem,
        out_shape=pltpu.VMEM((n_clusters, half), jnp.float32),
        compiler_params=pltpu.CompilerParams(vmem_limit_bytes=8 * MIB),
        cost_estimate=pl.CostEstimate(
            flops=2 * n_clusters * n_docs * half, bytes_accessed=2 * n_docs * (n_clusters + half), transcendentals=0
        ),
        name="own",
    )(core, plan, documents)


def sum_kernel(got_ref, out_ref):
    total = got_ref[0]
    for slot in range(1, got_ref.shape[0]):
        total += got_ref[slot]
    for slot in range(out_ref.shape[0]):
        out_ref[slot] = total


def sum_call(got, copies):
    vmem = pl.BlockSpec(memory_space=pltpu.VMEM)
    return pl.pallas_call(
        sum_kernel,
        in_specs=[vmem],
        out_specs=vmem,
        out_shape=pltpu.VMEM((copies, *got.shape[1:]), got.dtype),
        compiler_params=pltpu.CompilerParams(vmem_limit_bytes=4 * MIB),
        name="sum",
    )(got)


def pack_kernel(own_ref, got_ref, mass_ref, mass_got_ref, out_ref):
    half = own_ref.shape[1]
    n_slabs = out_ref.shape[0]
    slab = own_ref.shape[0] // n_slabs
    mass = mass_ref[0] + mass_got_ref[0]
    high = mass.astype(jnp.bfloat16)
    middle = (mass - high.astype(jnp.float32)).astype(jnp.bfloat16)
    low = (mass - high.astype(jnp.float32) - middle.astype(jnp.float32)).astype(jnp.bfloat16)
    rest = jnp.zeros((mass.shape[0], half - 3 * LANES), jnp.bfloat16)
    extra = jnp.concatenate([high, middle, low, rest], axis=1)
    for k in range(n_slabs):
        rows = slice(k * slab, (k + 1) * slab)
        out_ref[k, :slab, :] = (own_ref[rows, :] + got_ref[rows, :].astype(jnp.float32)).astype(jnp.bfloat16)
        out_ref[k, slab:, :] = extra


def pack_call(own, got, mass, mass_got):
    n_clusters, half = own.shape
    n_slabs = NX * NY
    vmem = pl.BlockSpec(memory_space=pltpu.VMEM)
    return pl.pallas_call(
        pack_kernel,
        in_specs=[vmem] * 4,
        out_specs=vmem,
        out_shape=pltpu.VMEM((n_slabs, n_clusters // n_slabs + mass.shape[1], half), jnp.bfloat16),
        compiler_params=pltpu.CompilerParams(vmem_limit_bytes=8 * MIB),
        name="pack",
    )(own, got, mass, mass_got)


def repack_kernel(slab, got_ref, out_ref):
    rows = slab // NZ
    total = got_ref[0].astype(jnp.float32)
    for k in range(1, got_ref.shape[0]):
        total += got_ref[k].astype(jnp.float32)
    half = total.shape[1]
    mass = total[slab:, :LANES] + total[slab:, LANES : 2 * LANES] + total[slab:, 2 * LANES : 3 * LANES]
    for k in range(NZ):
        out_ref[k, :, :half] = total[k * rows : (k + 1) * rows]
        out_ref[k, :, half:] = mass


def repack_call(got, slab):
    vmem = pl.BlockSpec(memory_space=pltpu.VMEM)
    return pl.pallas_call(
        functools.partial(repack_kernel, slab),
        in_specs=[vmem],
        out_specs=vmem,
        out_shape=pltpu.VMEM((NZ, slab // NZ, got.shape[2] + LANES), jnp.float32),
        compiler_params=pltpu.CompilerParams(vmem_limit_bytes=8 * MIB),
        name="repack",
    )(got)


def finish_kernel(place_ref, got_ref, cluster_mass_ref, out_ref, duals_ref):
    total = got_ref[0]
    for k in range(1, got_ref.shape[0]):
        total += got_ref[k]
    half = out_ref.shape[2]
    mass = total[:, half:]
    duals_ref[...] = TAU * (jnp.log(cluster_mass_ref[...]) - jnp.log(mass))
    place = place_ref[0]
    group = place // LANES
    first = place - group * LANES
    row = lax.broadcasted_iota(jnp.int32, mass.shape, 0)
    lane = lax.broadcasted_iota(jnp.int32, mass.shape, 1)
    line = jnp.sum(jnp.where(row == group, mass, 0.0), axis=0, keepdims=True)
    mine = jnp.where(lane == row + first, jnp.broadcast_to(line, mass.shape), 0.0)
    own_mass = jnp.sum(mine, axis=1, keepdims=True)
    centroids = (total[:, :half] / own_mass).astype(jnp.bfloat16)
    for k in range(out_ref.shape[0]):
        out_ref[k] = centroids


def finish_call(got, cluster_mass, place):
    rows, half = got.shape[1], got.shape[2] - LANES
    vmem = pl.BlockSpec(memory_space=pltpu.VMEM)
    return pl.pallas_call(
        finish_kernel,
        in_specs=[pl.BlockSpec(memory_space=pltpu.SMEM), vmem, vmem],
        out_specs=[vmem, vmem],
        out_shape=[
            pltpu.VMEM((NX * NZ, rows, half), jnp.bfloat16),
            jax.ShapeDtypeStruct(cluster_mass.shape, jnp.float32),
        ],
        compiler_params=pltpu.CompilerParams(vmem_limit_bytes=8 * MIB),
        name="finish",
    )(place, got, cluster_mass)


def join_kernel(core_ref, block_ref, other_ref, out_ref):
    half = block_ref.shape[1]
    core = core_ref[0]
    out_ref[:, pl.ds(pl.multiple_of(core * half, half), half)] = block_ref[...]
    out_ref[:, pl.ds(pl.multiple_of((1 - core) * half, half), half)] = other_ref[...]


def join_call(core, block, other):
    rows, half = block.shape
    vmem = pl.BlockSpec(memory_space=pltpu.VMEM)
    return pl.pallas_call(
        join_kernel,
        in_specs=[pl.BlockSpec(memory_space=pltpu.SMEM), vmem, vmem],
        out_specs=vmem,
        out_shape=jax.ShapeDtypeStruct((rows, 2 * half), jnp.bfloat16),
        compiler_params=pltpu.CompilerParams(vmem_limit_bytes=8 * MIB),
        name="join",
    )(core, block, other)


def sum_all(copies):
    got = lax.all_to_all(copies, ("x", "y"), 0, 0, tiled=True)
    return lax.all_to_all(sum_call(got, NZ * NC), ("z", "c"), 0, 0, tiled=True)


def per_device(documents, centroids, cluster_mass):
    n_docs = documents.shape[0] * NX * NZ * NC * NY
    n_clusters = centroids.shape[0]
    half = documents.shape[1] // NC
    core = lax.axis_index("c")
    slab = n_clusters // (NX * NY)
    rows = slab // NZ
    place = (lax.axis_index("y") * NX + lax.axis_index("x")) * slab + lax.axis_index("z") * rows
    documents, core, place = lax.optimization_barrier((documents, core.reshape(1), place.reshape(1)))
    loga = -math.log2(n_docs)
    cluster_mass = cluster_mass.reshape(n_clusters // LANES, LANES)
    scores, mass, documents = first_call(documents, centroids, loga)
    mass = middle_call(scores, sum_all(mass), cluster_mass, loga)
    send, plan, mass = last_call(scores, sum_all(mass), cluster_mass, documents, core, loga)
    own = own_call(plan, documents, core)
    packed = pack_call(own, swap_cores(send), mass, swap_cores(mass))
    packed = repack_call(lax.all_to_all(packed, ("y", "x"), 0, 0, tiled=True), slab)
    packed = lax.all_to_all(packed, ("z",), 0, 0, tiled=True)
    mine, duals = finish_call(packed, cluster_mass, place)
    block = lax.all_to_all(mine, ("x", "z"), 0, 0, tiled=True).reshape(n_clusters // NY, half)
    return join_call(core, block, swap_cores(block)), duals.reshape(n_clusters)


def solution(mesh):
    grid = Mesh(mesh.devices.reshape(NX, NZ, NC, NY), AXES)
    return jax.shard_map(
        per_device,
        mesh=grid,
        in_specs=(P(AXES, None), P(), P()),
        out_specs=(P("y", None), P()),
        check_vma=False,
    )
```

```python
import functools
import math

import jax
import jax.numpy as jnp
from jax import lax
from jax.experimental import pallas as pl
from jax.experimental.pallas import tpu as pltpu
from jax.sharding import Mesh
from jax.sharding import PartitionSpec as P

D = 1024
TAU = 0.8
TEMP = 4.0
NX, NZ, NC, NY = 4, 8, 2, 4
AXES = ("x", "z", "c", "y")
LANES = 128
BLOCK = 512
CHUNK = 64
LOG2E = 1 / math.log(2)
MIB = 2**20


def swap_cores(value):
    return lax.ppermute(value, "c", [(0, 1), (1, 0)])


def fold(value, op):
    return op(value.reshape(value.shape[0] // 8, 8, value.shape[1]), axis=0)


def block_masses(scores_ref, columns, duals_ref, loga, emit):
    n_clusters = scores_ref.shape[0]
    width = columns.stop - columns.start

    def shifted(row):
        value = scores_ref[row : row + CHUNK, columns]
        if duals_ref is None:
            return value
        duals = duals_ref[row : row + CHUNK, :]
        return value + jnp.concatenate([duals] * (width // LANES), axis=1)

    top = fold(shifted(0), jnp.max)
    for row in range(CHUNK, n_clusters, CHUNK):
        top = jnp.maximum(top, fold(shifted(row), jnp.max))
    top = jnp.max(top, axis=0, keepdims=True)
    total = fold(jnp.exp2(shifted(0) - top), jnp.sum)
    for row in range(CHUNK, n_clusters, CHUNK):
        total += fold(jnp.exp2(shifted(row) - top), jnp.sum)
    lse = top + jnp.log2(jnp.sum(total, axis=0, keepdims=True))
    row_duals = TAU * (loga - lse)
    for row in range(0, n_clusters, CHUNK):
        emit(row, jnp.exp2(scores_ref[row : row + CHUNK, columns] + row_duals))


def add_lanes(acc, row, mass):
    total = mass[:, :LANES]
    for lane in range(LANES, mass.shape[1], LANES):
        total += mass[:, lane : lane + LANES]
    acc[row : row + CHUNK, :] += total


def column_sums(acc, out_ref):
    rows = [jnp.sum(acc[k : k + LANES, :].T, axis=0, keepdims=True) for k in range(0, acc.shape[0], LANES)]
    sums = jnp.concatenate(rows, axis=0)
    for slot in range(out_ref.shape[0]):
        out_ref[slot] = sums


def start_duals(got_ref, cluster_mass_ref, duals_col):
    column_mass = got_ref[0]
    for slot in range(1, got_ref.shape[0]):
        column_mass += got_ref[slot]
    duals = TAU * (jnp.log2(cluster_mass_ref[...]) - jnp.log2(column_mass))
    for k in range(duals.shape[0]):
        row = jnp.broadcast_to(duals[k : k + 1, :], (LANES, LANES))
        duals_col[k * LANES : (k + 1) * LANES, :] = row.T


def first_kernel(loga, docs_hbm, cent_hbm, scores_ref, mass_ref, docs_ref, cent_ref, acc, sems):
    n_blocks = scores_ref.shape[0]
    copies = [pltpu.make_async_copy(cent_hbm, cent_ref, sems.at[n_blocks])]
    for block in range(n_blocks):
        rows = pl.ds(block * BLOCK, BLOCK)
        copies.append(pltpu.make_async_copy(docs_hbm.at[rows], docs_ref.at[rows], sems.at[block]))
    copies[0].start()
    copies[1].start()
    acc[...] = jnp.zeros_like(acc)
    copies[0].wait()
    for block in range(n_blocks + 1):
        if block < n_blocks:
            copies[block + 1].wait()
            if block == 0:
                for copy in copies[2:]:
                    copy.start()
            scores_ref[block] = lax.dot_general(
                cent_ref[...],
                docs_ref[block * BLOCK : (block + 1) * BLOCK, :],
                (((1,), (1,)), ((), ())),
                preferred_element_type=jnp.float32,
            ) * (TEMP / math.sqrt(D) * LOG2E)
        if block > 0:
            block_masses(scores_ref.at[block - 1], slice(0, BLOCK), None, loga, functools.partial(add_lanes, acc))
    column_sums(acc, mass_ref)


def first_call(documents, centroids, loga):
    n_docs, dim = documents.shape
    n_clusters = centroids.shape[0]
    n_blocks = n_docs // BLOCK
    vmem = pl.BlockSpec(memory_space=pltpu.VMEM)
    return pl.pallas_call(
        functools.partial(first_kernel, loga),
        in_specs=[pl.BlockSpec(memory_space=pltpu.HBM)] * 2,
        out_specs=[vmem] * 3,
        out_shape=[
            pltpu.VMEM((n_blocks, n_clusters, BLOCK), jnp.float32),
            pltpu.VMEM((NX * NY, n_clusters // LANES, LANES), jnp.float32),
            pltpu.VMEM((n_docs, dim), jnp.bfloat16),
        ],
        scratch_shapes=[
            pltpu.VMEM((n_clusters, dim), jnp.bfloat16),
            pltpu.VMEM((n_clusters, LANES), jnp.float32),
            pltpu.SemaphoreType.DMA((n_blocks + 1,)),
        ],
        compiler_params=pltpu.CompilerParams(vmem_limit_bytes=50 * MIB),
        name="first",
    )(documents, centroids)


def middle_kernel(loga, scores_ref, got_ref, cluster_mass_ref, mass_ref, duals_col, acc):
    start_duals(got_ref, cluster_mass_ref, duals_col)
    acc[...] = jnp.zeros_like(acc)

    @pl.loop(0, scores_ref.shape[0])
    def _(block):
        block_masses(scores_ref.at[block], slice(0, BLOCK), duals_col, loga, functools.partial(add_lanes, acc))

    column_sums(acc, mass_ref)


def middle_call(scores, got, cluster_mass, loga):
    n_clusters = scores.shape[1]
    vmem = pl.BlockSpec(memory_space=pltpu.VMEM)
    return pl.pallas_call(
        functools.partial(middle_kernel, loga),
        in_specs=[vmem] * 3,
        out_specs=vmem,
        out_shape=pltpu.VMEM((NX * NY, n_clusters // LANES, LANES), jnp.float32),
        scratch_shapes=[
            pltpu.VMEM((n_clusters, LANES), jnp.float32),
            pltpu.VMEM((n_clusters, LANES), jnp.float32),
        ],
        compiler_params=pltpu.CompilerParams(vmem_limit_bytes=8 * MIB),
        name="middle",
    )(scores, got, cluster_mass)


def columns_of(index, width):
    return pl.ds(pl.multiple_of(index * width, width), width)


def last_kernel(loga, core_ref, scores_ref, got_ref, cluster_mass_ref, docs_ref, send_a_ref, send_b_ref, plan_ref, mass_ref, total, duals_col, acc):
    n_blocks = scores_ref.shape[0]
    columns = columns_of(1 - core_ref[0], total.shape[1])
    start_duals(got_ref, cluster_mass_ref, duals_col)
    acc[...] = jnp.zeros_like(acc)
    for block in range(n_blocks + 1):
        if block > 0:
            rows = slice((block - 1) * BLOCK, block * BLOCK)
            part = lax.dot_general(
                plan_ref[:, rows], docs_ref[rows, columns], (((1,), (0,)), ((), ())), preferred_element_type=jnp.float32
            )
            if block > 1:
                part += total[...]
            if block < n_blocks:
                total[...] = part
            else:
                part = part.astype(jnp.bfloat16)
                send_a_ref[...] = part[:, : part.shape[1] // 2]
                send_b_ref[...] = part[:, part.shape[1] // 2 :]
        if block < n_blocks:

            def emit(row, mass, start=block * BLOCK):
                add_lanes(acc, row, mass)
                plan_ref[row : row + CHUNK, start : start + BLOCK] = mass.astype(jnp.bfloat16)

            block_masses(scores_ref.at[block], slice(0, BLOCK), duals_col, loga, emit)
    column_sums(acc, mass_ref)


def last_call(scores, got, cluster_mass, documents, core, loga):
    n_clusters = scores.shape[1]
    n_docs, dim = documents.shape
    half = dim // NC
    vmem = pl.BlockSpec(memory_space=pltpu.VMEM)
    return pl.pallas_call(
        functools.partial(last_kernel, loga),
        in_specs=[pl.BlockSpec(memory_space=pltpu.SMEM)] + [vmem] * 4,
        out_specs=[vmem] * 4,
        out_shape=[
            pltpu.VMEM((n_clusters, half // 2), jnp.bfloat16),
            pltpu.VMEM((n_clusters, half // 2), jnp.bfloat16),
            pltpu.VMEM((n_clusters, n_docs), jnp.bfloat16),
            pltpu.VMEM((1, n_clusters // LANES, LANES), jnp.float32),
        ],
        scratch_shapes=[
            pltpu.VMEM((n_clusters, half), jnp.float32),
            pltpu.VMEM((n_clusters, LANES), jnp.float32),
            pltpu.VMEM((n_clusters, LANES), jnp.float32),
        ],
        compiler_params=pltpu.CompilerParams(vmem_limit_bytes=16 * MIB),
        name="last",
    )(core, scores, got, cluster_mass, documents)


def own_kernel(part, core_ref, plan_ref, docs_ref, own_ref):
    width = own_ref.shape[1]
    own_ref[...] = lax.dot_general(
        plan_ref[...],
        docs_ref[:, columns_of(2 * core_ref[0] + part, width)],
        (((1,), (0,)), ((), ())),
        preferred_element_type=jnp.float32,
    )


def own_call(plan, documents, core, part):
    n_clusters, n_docs = plan.shape
    width = documents.shape[1] // NC // 2
    vmem = pl.BlockSpec(memory_space=pltpu.VMEM)
    return pl.pallas_call(
        functools.partial(own_kernel, part),
        in_specs=[pl.BlockSpec(memory_space=pltpu.SMEM), vmem, vmem],
        out_specs=vmem,
        out_shape=pltpu.VMEM((n_clusters, width), jnp.float32),
        compiler_params=pltpu.CompilerParams(vmem_limit_bytes=8 * MIB),
        cost_estimate=pl.CostEstimate(
            flops=2 * n_clusters * n_docs * width, bytes_accessed=2 * n_docs * (n_clusters + width), transcendentals=0
        ),
        name="own",
    )(core, plan, documents)


def sum_kernel(got_ref, out_ref):
    total = got_ref[0]
    for slot in range(1, got_ref.shape[0]):
        total += got_ref[slot]
    for slot in range(out_ref.shape[0]):
        out_ref[slot] = total


def sum_call(got, copies):
    vmem = pl.BlockSpec(memory_space=pltpu.VMEM)
    return pl.pallas_call(
        sum_kernel,
        in_specs=[vmem],
        out_specs=vmem,
        out_shape=pltpu.VMEM((copies, *got.shape[1:]), got.dtype),
        compiler_params=pltpu.CompilerParams(vmem_limit_bytes=4 * MIB),
        name="sum",
    )(got)


def spread_mass(mass):
    high = mass.astype(jnp.bfloat16)
    low = (mass - high.astype(jnp.float32)).astype(jnp.bfloat16)
    return jnp.concatenate([high, low], axis=1)


def gather_mass(pieces):
    return pieces[:, :LANES] + pieces[:, LANES:]


def pieces_kernel(n_parts, n_outer, has_mass, place_ref, *refs):
    parts, refs = refs[:n_parts], refs[n_parts:]
    masses_in, outs = refs[: len(refs) - NX], refs[len(refs) - NX :]
    n_clusters = parts[0].shape[0] - (8 if has_mass and not masses_in else 0)
    piece = n_clusters // (n_outer * NX)

    def total(rows):
        values = [part[rows, :].astype(jnp.float32) for part in parts]
        while len(values) > 1:
            values = [a + b for a, b in zip(values[::2], values[1::2])]
        return values[0]

    if masses_in:
        mass = spread_mass(masses_in[0][0] + masses_in[1][0])
    elif has_mass:
        mass = spread_mass(gather_mass(total(slice(n_clusters, n_clusters + 8))))
    for distance, out_ref in enumerate(outs):
        member = place_ref[0] ^ distance
        for outer in range(n_outer):
            rows = pl.ds(pl.multiple_of((outer * NX + member) * piece, piece), piece)
            out_ref[outer * piece : (outer + 1) * piece, :] = total(rows).astype(out_ref.dtype)
        if has_mass:
            out_ref[n_outer * piece :, :] = mass.astype(out_ref.dtype)


def pieces_call(place, parts, n_clusters, n_outer, has_mass, masses_in, name):
    width = parts[0].shape[1]
    shape = (n_clusters // NX + (8 if has_mass else 0), width)
    vmem = pl.BlockSpec(memory_space=pltpu.VMEM)
    return pl.pallas_call(
        functools.partial(pieces_kernel, len(parts), n_outer, has_mass),
        in_specs=[pl.BlockSpec(memory_space=pltpu.SMEM)] + [vmem] * (len(parts) + len(masses_in)),
        out_specs=[vmem] * NX,
        out_shape=[pltpu.VMEM(shape, jnp.float32)] + [pltpu.VMEM(shape, jnp.bfloat16)] * (NX - 1),
        compiler_params=pltpu.CompilerParams(vmem_limit_bytes=8 * MIB),
        name=name,
    )(place, *parts, *masses_in)


def exchange(pieces, axis):
    got = [pieces[0]]
    for distance in range(1, NX):
        got.append(lax.ppermute(pieces[distance], axis, [(i, i ^ distance) for i in range(NX)]))
    return got


def repack_kernel(*refs):
    parts_a, parts_b, out_ref = refs[:NX], refs[NX : 2 * NX], refs[2 * NX]

    def total(parts):
        values = [part[...].astype(jnp.float32) for part in parts]
        return (values[0] + values[1]) + (values[2] + values[3])

    total_a, total_b = total(parts_a), total(parts_b)
    slab, width = total_b.shape
    rows = slab // NZ
    mass = gather_mass(total_a[slab:])
    for k in range(NZ):
        out_ref[k, :, :width] = total_a[k * rows : (k + 1) * rows]
        out_ref[k, :, width : 2 * width] = total_b[k * rows : (k + 1) * rows]
        out_ref[k, :, 2 * width :] = mass


def repack_call(parts_a, parts_b):
    slab, width = parts_b[0].shape
    vmem = pl.BlockSpec(memory_space=pltpu.VMEM)
    return pl.pallas_call(
        repack_kernel,
        in_specs=[vmem] * (2 * NX),
        out_specs=vmem,
        out_shape=pltpu.VMEM((NZ, slab // NZ, 2 * width + LANES), jnp.float32),
        compiler_params=pltpu.CompilerParams(vmem_limit_bytes=8 * MIB),
        name="repack",
    )(*parts_a, *parts_b)


def finish_kernel(place_ref, got_ref, cluster_mass_ref, out_ref, duals_ref):
    total = got_ref[0]
    for k in range(1, got_ref.shape[0]):
        total += got_ref[k]
    half = out_ref.shape[2]
    mass = total[:, half:]
    duals_ref[...] = TAU * (jnp.log(cluster_mass_ref[...]) - jnp.log(mass))
    place = place_ref[0]
    group = place // LANES
    first = place - group * LANES
    row = lax.broadcasted_iota(jnp.int32, mass.shape, 0)
    lane = lax.broadcasted_iota(jnp.int32, mass.shape, 1)
    line = jnp.sum(jnp.where(row == group, mass, 0.0), axis=0, keepdims=True)
    mine = jnp.where(lane == row + first, jnp.broadcast_to(line, mass.shape), 0.0)
    own_mass = jnp.sum(mine, axis=1, keepdims=True)
    centroids = (total[:, :half] / own_mass).astype(jnp.bfloat16)
    for k in range(out_ref.shape[0]):
        out_ref[k] = centroids


def finish_call(got, cluster_mass, place):
    rows, half = got.shape[1], got.shape[2] - LANES
    vmem = pl.BlockSpec(memory_space=pltpu.VMEM)
    return pl.pallas_call(
        finish_kernel,
        in_specs=[pl.BlockSpec(memory_space=pltpu.SMEM), vmem, vmem],
        out_specs=[vmem, vmem],
        out_shape=[
            pltpu.VMEM((NX * NZ, rows, half), jnp.bfloat16),
            jax.ShapeDtypeStruct(cluster_mass.shape, jnp.float32),
        ],
        compiler_params=pltpu.CompilerParams(vmem_limit_bytes=8 * MIB),
        name="finish",
    )(place, got, cluster_mass)


def join_kernel(core_ref, block_ref, other_ref, out_ref):
    half = block_ref.shape[1]
    core = core_ref[0]
    out_ref[:, pl.ds(pl.multiple_of(core * half, half), half)] = block_ref[...]
    out_ref[:, pl.ds(pl.multiple_of((1 - core) * half, half), half)] = other_ref[...]


def join_call(core, block, other):
    rows, half = block.shape
    vmem = pl.BlockSpec(memory_space=pltpu.VMEM)
    return pl.pallas_call(
        join_kernel,
        in_specs=[pl.BlockSpec(memory_space=pltpu.SMEM), vmem, vmem],
        out_specs=vmem,
        out_shape=jax.ShapeDtypeStruct((rows, 2 * half), jnp.bfloat16),
        compiler_params=pltpu.CompilerParams(vmem_limit_bytes=8 * MIB),
        name="join",
    )(core, block, other)


def sum_all(copies):
    got = lax.all_to_all(copies, ("x", "y"), 0, 0, tiled=True)
    return lax.all_to_all(sum_call(got, NZ * NC), ("z", "c"), 0, 0, tiled=True)


def per_device(documents, centroids, cluster_mass):
    n_docs = documents.shape[0] * NX * NZ * NC * NY
    n_clusters = centroids.shape[0]
    half = documents.shape[1] // NC
    core = lax.axis_index("c")
    slab = n_clusters // (NX * NY)
    rows = slab // NZ
    place = (lax.axis_index("y") * NX + lax.axis_index("x")) * slab + lax.axis_index("z") * rows
    along_x, along_y = lax.axis_index("x").reshape(1), lax.axis_index("y").reshape(1)
    documents, core, place, along_x, along_y = lax.optimization_barrier(
        (documents, core.reshape(1), place.reshape(1), along_x, along_y)
    )
    loga = -math.log2(n_docs)
    cluster_mass = cluster_mass.reshape(n_clusters // LANES, LANES)
    scores, mass, documents = first_call(documents, centroids, loga)
    mass = middle_call(scores, sum_all(mass), cluster_mass, loga)
    send_a, send_b, plan, mass = last_call(scores, sum_all(mass), cluster_mass, documents, core, loga)
    got_a, mass_got, got_b = swap_cores(send_a), swap_cores(mass), swap_cores(send_b)
    own = own_call(plan, documents, core, 0)
    part_a = pieces_call(along_y, [own, got_a], n_clusters, 1, True, [mass, mass_got], "pack_a")
    part_a = exchange(part_a, "y")
    own = own_call(plan, documents, core, 1)
    part_b = pieces_call(along_x, [own, got_b], n_clusters, NY, False, [], "pack_b")
    part_b = exchange(part_b, "x")
    part_a = exchange(pieces_call(along_x, part_a, n_clusters // NY, 1, True, [], "mid_a"), "x")
    part_b = exchange(pieces_call(along_y, part_b, n_clusters // NX, 1, False, [], "mid_b"), "y")
    packed = repack_call(part_a, part_b)
    packed = lax.all_to_all(packed, ("z",), 0, 0, tiled=True)
    mine, duals = finish_call(packed, cluster_mass, place)
    block = lax.all_to_all(mine, ("x", "z"), 0, 0, tiled=True).reshape(n_clusters // NY, half)
    return join_call(core, block, swap_cores(block)), duals.reshape(n_clusters)


def solution(mesh):
    grid = Mesh(mesh.devices.reshape(NX, NZ, NC, NY), AXES)
    return jax.shard_map(
        per_device,
        mesh=grid,
        in_specs=(P(AXES, None), P(), P()),
        out_specs=(P("y", None), P()),
        check_vma=False,
    )
```

```python
import functools
import math

import jax
import jax.numpy as jnp
from jax import lax
from jax.experimental import pallas as pl
from jax.experimental.pallas import tpu as pltpu
from jax.sharding import Mesh
from jax.sharding import PartitionSpec as P

D = 1024
TAU = 0.8
TEMP = 4.0
NX, NZ, NC, NY = 4, 8, 2, 4
AXES = ("x", "z", "c", "y")
LANES = 128
BLOCK = 512
GROUP = 2
CHUNK = 64
LOG2E = 1 / math.log(2)
MIB = 2**20


def swap_cores(value):
    return lax.ppermute(value, "c", [(0, 1), (1, 0)])


def fold(value, op):
    return op(value.reshape(value.shape[0] // 8, 8, value.shape[1]), axis=0)


def block_masses(scores_ref, columns, duals_ref, loga, emit):
    n_clusters = scores_ref.shape[0]
    width = columns.stop - columns.start

    def shifted(row):
        value = scores_ref[row : row + CHUNK, columns]
        if duals_ref is None:
            return value
        duals = duals_ref[row : row + CHUNK, :]
        return value + jnp.concatenate([duals] * (width // LANES), axis=1)

    top = fold(shifted(0), jnp.max)
    for row in range(CHUNK, n_clusters, CHUNK):
        top = jnp.maximum(top, fold(shifted(row), jnp.max))
    top = jnp.max(top, axis=0, keepdims=True)
    total = fold(jnp.exp2(shifted(0) - top), jnp.sum)
    for row in range(CHUNK, n_clusters, CHUNK):
        total += fold(jnp.exp2(shifted(row) - top), jnp.sum)
    lse = top + jnp.log2(jnp.sum(total, axis=0, keepdims=True))
    row_duals = TAU * (loga - lse)
    for row in range(0, n_clusters, CHUNK):
        emit(row, jnp.exp2(scores_ref[row : row + CHUNK, columns] + row_duals))


def add_lanes(acc, row, mass):
    total = mass[:, :LANES]
    for lane in range(LANES, mass.shape[1], LANES):
        total += mass[:, lane : lane + LANES]
    acc[row : row + CHUNK, :] += total


def column_sums(acc, out_ref):
    rows = [jnp.sum(acc[k : k + LANES, :].T, axis=0, keepdims=True) for k in range(0, acc.shape[0], LANES)]
    sums = jnp.concatenate(rows, axis=0).astype(out_ref.dtype)
    for slot in range(out_ref.shape[0]):
        out_ref[slot] = sums


def sum_slots(got_ref):
    total = got_ref[0].astype(jnp.float32)
    for slot in range(1, got_ref.shape[0]):
        total += got_ref[slot].astype(jnp.float32)
    return total


def start_duals(got_ref, cluster_mass_ref, duals_col):
    column_mass = sum_slots(got_ref)
    duals = TAU * (jnp.log2(cluster_mass_ref[...]) - jnp.log2(column_mass))
    for k in range(duals.shape[0]):
        row = jnp.broadcast_to(duals[k : k + 1, :], (LANES, LANES))
        duals_col[k * LANES : (k + 1) * LANES, :] = row.T


def first_kernel(loga, docs_hbm, cent_hbm, scores_ref, mass_ref, docs_ref, cent_ref, acc, sems):
    n_blocks = scores_ref.shape[0]
    copies = [pltpu.make_async_copy(cent_hbm, cent_ref, sems.at[n_blocks])]
    for block in range(n_blocks):
        rows = pl.ds(block * BLOCK, BLOCK)
        copies.append(pltpu.make_async_copy(docs_hbm.at[rows], docs_ref.at[rows], sems.at[block]))
    for copy in copies[: 1 + GROUP]:
        copy.start()
    acc[...] = jnp.zeros_like(acc)
    copies[0].wait()
    for block in range(n_blocks + 1):
        if block % GROUP == 0 and block < n_blocks:
            for k in range(block, block + GROUP):
                copies[k + 1].wait()
            if block == 0:
                for copy in copies[1 + GROUP :]:
                    copy.start()
            scores = lax.dot_general(
                cent_ref[...],
                docs_ref[block * BLOCK : (block + GROUP) * BLOCK, :],
                (((1,), (1,)), ((), ())),
                preferred_element_type=jnp.float32,
            ) * (TEMP / math.sqrt(D) * LOG2E)
            for k in range(GROUP):
                scores_ref[block + k] = scores[:, k * BLOCK : (k + 1) * BLOCK]
        if block > 0:
            block_masses(scores_ref.at[block - 1], slice(0, BLOCK), None, loga, functools.partial(add_lanes, acc))
    column_sums(acc, mass_ref)


def first_call(documents, centroids, loga):
    n_docs, dim = documents.shape
    n_clusters = centroids.shape[0]
    n_blocks = n_docs // BLOCK
    vmem = pl.BlockSpec(memory_space=pltpu.VMEM)
    return pl.pallas_call(
        functools.partial(first_kernel, loga),
        in_specs=[pl.BlockSpec(memory_space=pltpu.HBM)] * 2,
        out_specs=[vmem] * 3,
        out_shape=[
            pltpu.VMEM((n_blocks, n_clusters, BLOCK), jnp.float32),
            pltpu.VMEM((NX * NY, n_clusters // LANES, LANES), jnp.bfloat16),
            pltpu.VMEM((n_docs, dim), jnp.bfloat16),
        ],
        scratch_shapes=[
            pltpu.VMEM((n_clusters, dim), jnp.bfloat16),
            pltpu.VMEM((n_clusters, LANES), jnp.float32),
            pltpu.SemaphoreType.DMA((n_blocks + 1,)),
        ],
        compiler_params=pltpu.CompilerParams(vmem_limit_bytes=50 * MIB),
        name="first",
    )(documents, centroids)


def middle_kernel(loga, scores_ref, got_ref, cluster_mass_ref, mass_ref, duals_col, acc):
    start_duals(got_ref, cluster_mass_ref, duals_col)
    acc[...] = jnp.zeros_like(acc)

    @pl.loop(0, scores_ref.shape[0])
    def _(block):
        block_masses(scores_ref.at[block], slice(0, BLOCK), duals_col, loga, functools.partial(add_lanes, acc))

    column_sums(acc, mass_ref)


def middle_call(scores, got, cluster_mass, loga):
    n_clusters = scores.shape[1]
    vmem = pl.BlockSpec(memory_space=pltpu.VMEM)
    return pl.pallas_call(
        functools.partial(middle_kernel, loga),
        in_specs=[vmem] * 3,
        out_specs=vmem,
        out_shape=pltpu.VMEM((NX * NY, n_clusters // LANES, LANES), jnp.bfloat16),
        scratch_shapes=[
            pltpu.VMEM((n_clusters, LANES), jnp.float32),
            pltpu.VMEM((n_clusters, LANES), jnp.float32),
        ],
        compiler_params=pltpu.CompilerParams(vmem_limit_bytes=8 * MIB),
        name="middle",
    )(scores, got, cluster_mass)


def half_columns(core, half):
    return pl.ds(pl.multiple_of(core * half, half), half)


def last_kernel(loga, core_ref, scores_ref, got_ref, cluster_mass_ref, docs_ref, send_ref, plan_ref, mass_ref, total, duals_col, acc):
    n_blocks = scores_ref.shape[0]
    columns = half_columns(1 - core_ref[0], send_ref.shape[1])
    start_duals(got_ref, cluster_mass_ref, duals_col)
    acc[...] = jnp.zeros_like(acc)
    for block in range(n_blocks + 1):
        if block > 0:
            rows = slice((block - 1) * BLOCK, block * BLOCK)
            part = lax.dot_general(
                plan_ref[:, rows], docs_ref[rows, columns], (((1,), (0,)), ((), ())), preferred_element_type=jnp.float32
            )
            if block > 1:
                part += total[...]
            if block < n_blocks:
                total[...] = part
            else:
                send_ref[...] = part.astype(jnp.bfloat16)
        if block < n_blocks:

            def emit(row, mass, start=block * BLOCK):
                add_lanes(acc, row, mass)
                plan_ref[row : row + CHUNK, start : start + BLOCK] = mass.astype(jnp.bfloat16)

            block_masses(scores_ref.at[block], slice(0, BLOCK), duals_col, loga, emit)
    column_sums(acc, mass_ref)


def last_call(scores, got, cluster_mass, documents, core, loga):
    n_clusters = scores.shape[1]
    n_docs, dim = documents.shape
    half = dim // NC
    vmem = pl.BlockSpec(memory_space=pltpu.VMEM)
    return pl.pallas_call(
        functools.partial(last_kernel, loga),
        in_specs=[pl.BlockSpec(memory_space=pltpu.SMEM)] + [vmem] * 4,
        out_specs=[vmem] * 3,
        out_shape=[
            pltpu.VMEM((n_clusters, half), jnp.bfloat16),
            pltpu.VMEM((n_clusters, n_docs), jnp.bfloat16),
            pltpu.VMEM((1, n_clusters // LANES, LANES), jnp.float32),
        ],
        scratch_shapes=[
            pltpu.VMEM((n_clusters, half), jnp.float32),
            pltpu.VMEM((n_clusters, LANES), jnp.float32),
            pltpu.VMEM((n_clusters, LANES), jnp.float32),
        ],
        compiler_params=pltpu.CompilerParams(vmem_limit_bytes=16 * MIB),
        name="last",
    )(core, scores, got, cluster_mass, documents)


def own_kernel(core_ref, plan_ref, docs_ref, own_ref):
    half = own_ref.shape[1]
    own_ref[...] = lax.dot_general(
        plan_ref[...],
        docs_ref[:, half_columns(core_ref[0], half)],
        (((1,), (0,)), ((), ())),
        preferred_element_type=jnp.float32,
    )


def own_call(plan, documents, core):
    n_clusters, n_docs = plan.shape
    half = documents.shape[1] // NC
    vmem = pl.BlockSpec(memory_space=pltpu.VMEM)
    return pl.pallas_call(
        own_kernel,
        in_specs=[pl.BlockSpec(memory_space=pltpu.SMEM), vmem, vmem],
        out_specs=vmem,
        out_shape=pltpu.VMEM((n_clusters, half), jnp.float32),
        compiler_params=pltpu.CompilerParams(vmem_limit_bytes=8 * MIB),
        cost_estimate=pl.CostEstimate(
            flops=2 * n_clusters * n_docs * half, bytes_accessed=2 * n_docs * (n_clusters + half), transcendentals=0
        ),
        name="own",
    )(core, plan, documents)


def sum_kernel(got_ref, out_ref):
    total = sum_slots(got_ref).astype(out_ref.dtype)
    for slot in range(out_ref.shape[0]):
        out_ref[slot] = total


def sum_call(got, copies):
    vmem = pl.BlockSpec(memory_space=pltpu.VMEM)
    return pl.pallas_call(
        sum_kernel,
        in_specs=[vmem],
        out_specs=vmem,
        out_shape=pltpu.VMEM((copies, *got.shape[1:]), got.dtype),
        compiler_params=pltpu.CompilerParams(vmem_limit_bytes=4 * MIB),
        name="sum",
    )(got)


def pack_kernel(own_ref, got_ref, mass_ref, mass_got_ref, out_ref):
    n_slabs = out_ref.shape[0]
    slab = own_ref.shape[0] // n_slabs
    mass = mass_ref[0] + mass_got_ref[0]
    high = mass.astype(jnp.bfloat16)
    low = (mass - high.astype(jnp.float32)).astype(jnp.bfloat16)
    for k in range(n_slabs):
        rows = slice(k * slab, (k + 1) * slab)
        total = (own_ref[rows, :] + got_ref[rows, :].astype(jnp.float32)).astype(jnp.bfloat16)
        pieces = [total[:, lane : lane + LANES] for lane in range(0, own_ref.shape[1], LANES)] + [high, low]
        first = 0
        for piece in pieces:
            out_ref[k, first : first + piece.shape[0], :] = piece
            first += piece.shape[0]


def pack_call(own, got, mass, mass_got):
    n_clusters, half = own.shape
    n_slabs = NX * NY
    rows = n_clusters // n_slabs * (half // LANES) + 2 * mass.shape[1]
    vmem = pl.BlockSpec(memory_space=pltpu.VMEM)
    return pl.pallas_call(
        pack_kernel,
        in_specs=[vmem] * 4,
        out_specs=vmem,
        out_shape=pltpu.VMEM((n_slabs, rows, LANES), jnp.bfloat16),
        compiler_params=pltpu.CompilerParams(vmem_limit_bytes=8 * MIB),
        name="pack",
    )(own, got, mass, mass_got)


def repack_kernel(slab, got_ref, out_ref):
    groups = out_ref.shape[2] // LANES - 1
    rows = slab // NZ
    total = sum_slots(got_ref)
    mass = total[groups * slab : groups * slab + 8] + total[groups * slab + 8 :]
    for k in range(NZ):
        for group in range(groups):
            first = group * slab + k * rows
            out_ref[k, :, group * LANES : (group + 1) * LANES] = total[first : first + rows]
        out_ref[k, :, groups * LANES :] = mass


def repack_call(got, slab):
    groups = (got.shape[1] - 16) // slab
    vmem = pl.BlockSpec(memory_space=pltpu.VMEM)
    return pl.pallas_call(
        functools.partial(repack_kernel, slab),
        in_specs=[vmem],
        out_specs=vmem,
        out_shape=pltpu.VMEM((NZ, slab // NZ, (groups + 1) * LANES), jnp.float32),
        compiler_params=pltpu.CompilerParams(vmem_limit_bytes=8 * MIB),
        name="repack",
    )(got)


def finish_kernel(place_ref, got_ref, cluster_mass_ref, out_ref, duals_ref):
    total = sum_slots(got_ref)
    half = out_ref.shape[2]
    mass = total[:, half:]
    duals_ref[...] = TAU * (jnp.log(cluster_mass_ref[...]) - jnp.log(mass))
    place = place_ref[0]
    group = place // LANES
    first = place - group * LANES
    row = lax.broadcasted_iota(jnp.int32, mass.shape, 0)
    lane = lax.broadcasted_iota(jnp.int32, mass.shape, 1)
    line = jnp.sum(jnp.where(row == group, mass, 0.0), axis=0, keepdims=True)
    mine = jnp.where(lane == row + first, jnp.broadcast_to(line, mass.shape), 0.0)
    own_mass = jnp.sum(mine, axis=1, keepdims=True)
    centroids = (total[:, :half] / own_mass).astype(jnp.bfloat16)
    for k in range(out_ref.shape[0]):
        out_ref[k] = centroids


def finish_call(got, cluster_mass, place):
    rows, half = got.shape[1], got.shape[2] - LANES
    vmem = pl.BlockSpec(memory_space=pltpu.VMEM)
    return pl.pallas_call(
        finish_kernel,
        in_specs=[pl.BlockSpec(memory_space=pltpu.SMEM), vmem, vmem],
        out_specs=[vmem, vmem],
        out_shape=[
            pltpu.VMEM((NX * NZ, rows, half), jnp.bfloat16),
            pltpu.VMEM(cluster_mass.shape, jnp.float32),
        ],
        compiler_params=pltpu.CompilerParams(vmem_limit_bytes=8 * MIB),
        name="finish",
    )(place, got, cluster_mass)


def write_kernel(core_ref, half_ref, *refs):
    out_hbm, sem = refs[-2:]
    half = half_ref.shape[1]
    columns = pl.ds(pl.multiple_of(core_ref[0] * half, half), half)
    copy = pltpu.make_async_copy(half_ref, out_hbm.at[:, columns], sem)
    copy.start()
    copy.wait()


def write_call(core, half, out):
    rows, width = half.shape
    hbm = pl.BlockSpec(memory_space=pltpu.HBM)
    specs = [pl.BlockSpec(memory_space=pltpu.SMEM), pl.BlockSpec(memory_space=pltpu.VMEM)]
    operands = (core, half) if out is None else (core, half, out)
    return pl.pallas_call(
        write_kernel,
        in_specs=specs + [hbm] * (len(operands) - 2),
        out_specs=hbm,
        out_shape=jax.ShapeDtypeStruct((rows, 2 * width), half.dtype),
        scratch_shapes=[pltpu.SemaphoreType.DMA],
        input_output_aliases={} if out is None else {2: 0},
        compiler_params=pltpu.CompilerParams(vmem_limit_bytes=4 * MIB),
        cost_estimate=pl.CostEstimate(flops=0, bytes_accessed=8 * rows * width, transcendentals=0),
        name="write",
    )(*operands)


def sum_all(copies):
    got = lax.all_to_all(copies, ("x", "y"), 0, 0, tiled=True)
    return lax.all_to_all(sum_call(got, NZ * NC), ("z", "c"), 0, 0, tiled=True)


def per_device(documents, centroids, cluster_mass):
    n_docs = documents.shape[0] * NX * NZ * NC * NY
    n_clusters = centroids.shape[0]
    half = documents.shape[1] // NC
    core = lax.axis_index("c")
    slab = n_clusters // (NX * NY)
    rows = slab // NZ
    place = (lax.axis_index("y") * NX + lax.axis_index("x")) * slab + lax.axis_index("z") * rows
    documents, core, place = lax.optimization_barrier((documents, core.reshape(1), place.reshape(1)))
    loga = -math.log2(n_docs)
    cluster_mass = cluster_mass.reshape(n_clusters // LANES, LANES)
    scores, mass, documents = first_call(documents, centroids, loga)
    mass = middle_call(scores, sum_all(mass), cluster_mass, loga)
    send, plan, mass = last_call(scores, sum_all(mass), cluster_mass, documents, core, loga)
    own = own_call(plan, documents, core)
    packed = pack_call(own, swap_cores(send), mass, swap_cores(mass))
    packed = repack_call(lax.all_to_all(packed, ("y", "x"), 0, 0, tiled=True), slab)
    packed = lax.all_to_all(packed, ("z",), 0, 0, tiled=True)
    mine, duals = finish_call(packed, cluster_mass, place)
    block = lax.all_to_all(mine, ("x", "z"), 0, 0, tiled=True).reshape(n_clusters // NY, half)
    other = swap_cores(block)
    out = write_call(core, block, None)
    return write_call(1 - core, other, out), duals.reshape(n_clusters)


def solution(mesh):
    grid = Mesh(mesh.devices.reshape(NX, NZ, NC, NY), AXES)
    return jax.shard_map(
        per_device,
        mesh=grid,
        in_specs=(P(AXES, None), P(), P()),
        out_specs=(P("y", None), P()),
        check_vma=False,
    )
```

```python
import functools
import math

import jax
import jax.numpy as jnp
from jax import lax
from jax.experimental import pallas as pl
from jax.experimental.pallas import tpu as pltpu
from jax.sharding import Mesh
from jax.sharding import PartitionSpec as P

D = 1024
TAU = 0.8
TEMP = 4.0
NX, NZ, NC, NY = 4, 8, 2, 4
AXES = ("x", "z", "c", "y")
LANES = 128
BLOCK = 512
GROUP = 2
CHUNK = 64
LOG2E = 1 / math.log(2)
MIB = 2**20


def swap_cores(value):
    return lax.ppermute(value, "c", [(0, 1), (1, 0)])


def fold(value, op):
    return op(value.reshape(value.shape[0] // 8, 8, value.shape[1]), axis=0)


def block_masses(scores_ref, columns, duals_ref, loga, emit):
    n_clusters = scores_ref.shape[0]
    width = columns.stop - columns.start

    def shifted(row):
        value = scores_ref[row : row + CHUNK, columns]
        if duals_ref is None:
            return value
        duals = duals_ref[row : row + CHUNK, :]
        return value + jnp.concatenate([duals] * (width // LANES), axis=1)

    top = fold(shifted(0), jnp.max)
    for row in range(CHUNK, n_clusters, CHUNK):
        top = jnp.maximum(top, fold(shifted(row), jnp.max))
    top = jnp.max(top, axis=0, keepdims=True)
    total = fold(jnp.exp2(shifted(0) - top), jnp.sum)
    for row in range(CHUNK, n_clusters, CHUNK):
        total += fold(jnp.exp2(shifted(row) - top), jnp.sum)
    lse = top + jnp.log2(jnp.sum(total, axis=0, keepdims=True))
    row_duals = TAU * (loga - lse)
    for row in range(0, n_clusters, CHUNK):
        emit(row, jnp.exp2(scores_ref[row : row + CHUNK, columns] + row_duals))


def add_lanes(acc, row, mass):
    total = mass[:, :LANES]
    for lane in range(LANES, mass.shape[1], LANES):
        total += mass[:, lane : lane + LANES]
    acc[row : row + CHUNK, :] += total


def column_sums(acc, out_ref):
    rows = [jnp.sum(acc[k : k + LANES, :].T, axis=0, keepdims=True) for k in range(0, acc.shape[0], LANES)]
    sums = jnp.concatenate(rows, axis=0).astype(out_ref.dtype)
    for slot in range(out_ref.shape[0]):
        out_ref[slot] = sums


def sum_slots(got_ref):
    total = got_ref[0].astype(jnp.float32)
    for slot in range(1, got_ref.shape[0]):
        total += got_ref[slot].astype(jnp.float32)
    return total


def start_duals(got_ref, cluster_mass_ref, duals_col):
    column_mass = sum_slots(got_ref)
    duals = TAU * (jnp.log2(cluster_mass_ref[...]) - jnp.log2(column_mass))
    for k in range(duals.shape[0]):
        row = jnp.broadcast_to(duals[k : k + 1, :], (LANES, LANES))
        duals_col[k * LANES : (k + 1) * LANES, :] = row.T


def first_kernel(loga, docs_hbm, cent_hbm, scores_ref, mass_ref, docs_ref, cent_ref, acc, sems):
    n_blocks = scores_ref.shape[0]
    copies = [pltpu.make_async_copy(cent_hbm, cent_ref, sems.at[n_blocks])]
    for block in range(n_blocks):
        rows = pl.ds(block * BLOCK, BLOCK)
        copies.append(pltpu.make_async_copy(docs_hbm.at[rows], docs_ref.at[rows], sems.at[block]))
    for copy in copies[: 1 + GROUP]:
        copy.start()
    acc[...] = jnp.zeros_like(acc)
    copies[0].wait()
    for block in range(n_blocks + 1):
        if block % GROUP == 0 and block < n_blocks:
            for k in range(block, block + GROUP):
                copies[k + 1].wait()
            if block == 0:
                for copy in copies[1 + GROUP :]:
                    copy.start()
            scores = lax.dot_general(
                cent_ref[...],
                docs_ref[block * BLOCK : (block + GROUP) * BLOCK, :],
                (((1,), (1,)), ((), ())),
                preferred_element_type=jnp.float32,
            ) * (TEMP / math.sqrt(D) * LOG2E)
            for k in range(GROUP):
                scores_ref[block + k] = scores[:, k * BLOCK : (k + 1) * BLOCK]
        if block > 0:
            block_masses(scores_ref.at[block - 1], slice(0, BLOCK), None, loga, functools.partial(add_lanes, acc))
    column_sums(acc, mass_ref)


def first_call(documents, centroids, loga):
    n_docs, dim = documents.shape
    n_clusters = centroids.shape[0]
    n_blocks = n_docs // BLOCK
    vmem = pl.BlockSpec(memory_space=pltpu.VMEM)
    return pl.pallas_call(
        functools.partial(first_kernel, loga),
        in_specs=[pl.BlockSpec(memory_space=pltpu.HBM)] * 2,
        out_specs=[vmem] * 3,
        out_shape=[
            pltpu.VMEM((n_blocks, n_clusters, BLOCK), jnp.float32),
            pltpu.VMEM((NX * NY, n_clusters // LANES, LANES), jnp.bfloat16),
            pltpu.VMEM((n_docs, dim), jnp.bfloat16),
        ],
        scratch_shapes=[
            pltpu.VMEM((n_clusters, dim), jnp.bfloat16),
            pltpu.VMEM((n_clusters, LANES), jnp.float32),
            pltpu.SemaphoreType.DMA((n_blocks + 1,)),
        ],
        compiler_params=pltpu.CompilerParams(vmem_limit_bytes=50 * MIB),
        name="first",
    )(documents, centroids)


def middle_kernel(loga, scores_ref, got_ref, cluster_mass_ref, mass_ref, duals_col, acc):
    start_duals(got_ref, cluster_mass_ref, duals_col)
    acc[...] = jnp.zeros_like(acc)

    @pl.loop(0, scores_ref.shape[0])
    def _(block):
        block_masses(scores_ref.at[block], slice(0, BLOCK), duals_col, loga, functools.partial(add_lanes, acc))

    column_sums(acc, mass_ref)


def middle_call(scores, got, cluster_mass, loga):
    n_clusters = scores.shape[1]
    vmem = pl.BlockSpec(memory_space=pltpu.VMEM)
    return pl.pallas_call(
        functools.partial(middle_kernel, loga),
        in_specs=[vmem] * 3,
        out_specs=vmem,
        out_shape=pltpu.VMEM((NX * NY, n_clusters // LANES, LANES), jnp.bfloat16),
        scratch_shapes=[
            pltpu.VMEM((n_clusters, LANES), jnp.float32),
            pltpu.VMEM((n_clusters, LANES), jnp.float32),
        ],
        compiler_params=pltpu.CompilerParams(vmem_limit_bytes=8 * MIB),
        name="middle",
    )(scores, got, cluster_mass)


def half_columns(core, half):
    return pl.ds(pl.multiple_of(core * half, half), half)


def last_kernel(loga, core_ref, scores_ref, got_ref, cluster_mass_ref, docs_ref, send_ref, plan_ref, mass_ref, total, duals_col, acc):
    n_blocks = scores_ref.shape[0]
    columns = half_columns(1 - core_ref[0], send_ref.shape[1])
    start_duals(got_ref, cluster_mass_ref, duals_col)
    acc[...] = jnp.zeros_like(acc)
    for block in range(n_blocks + 1):
        if block > 0:
            rows = slice((block - 1) * BLOCK, block * BLOCK)
            part = lax.dot_general(
                plan_ref[:, rows], docs_ref[rows, columns], (((1,), (0,)), ((), ())), preferred_element_type=jnp.float32
            )
            if block > 1:
                part += total[...]
            if block < n_blocks:
                total[...] = part
            else:
                send_ref[...] = part.astype(jnp.bfloat16)
        if block < n_blocks:

            def emit(row, mass, start=block * BLOCK):
                add_lanes(acc, row, mass)
                plan_ref[row : row + CHUNK, start : start + BLOCK] = mass.astype(jnp.bfloat16)

            block_masses(scores_ref.at[block], slice(0, BLOCK), duals_col, loga, emit)
    column_sums(acc, mass_ref)


def last_call(scores, got, cluster_mass, documents, core, loga):
    n_clusters = scores.shape[1]
    n_docs, dim = documents.shape
    half = dim // NC
    vmem = pl.BlockSpec(memory_space=pltpu.VMEM)
    return pl.pallas_call(
        functools.partial(last_kernel, loga),
        in_specs=[pl.BlockSpec(memory_space=pltpu.SMEM)] + [vmem] * 4,
        out_specs=[vmem] * 3,
        out_shape=[
            pltpu.VMEM((n_clusters, half), jnp.bfloat16),
            pltpu.VMEM((n_clusters, n_docs), jnp.bfloat16),
            pltpu.VMEM((1, n_clusters // LANES, LANES), jnp.float32),
        ],
        scratch_shapes=[
            pltpu.VMEM((n_clusters, half), jnp.float32),
            pltpu.VMEM((n_clusters, LANES), jnp.float32),
            pltpu.VMEM((n_clusters, LANES), jnp.float32),
        ],
        compiler_params=pltpu.CompilerParams(vmem_limit_bytes=16 * MIB),
        name="last",
    )(core, scores, got, cluster_mass, documents)


def own_kernel(core_ref, plan_ref, docs_ref, own_ref):
    half = own_ref.shape[1]
    own_ref[...] = lax.dot_general(
        plan_ref[...],
        docs_ref[:, half_columns(core_ref[0], half)],
        (((1,), (0,)), ((), ())),
        preferred_element_type=jnp.float32,
    )


def own_call(plan, documents, core):
    n_clusters, n_docs = plan.shape
    half = documents.shape[1] // NC
    vmem = pl.BlockSpec(memory_space=pltpu.VMEM)
    return pl.pallas_call(
        own_kernel,
        in_specs=[pl.BlockSpec(memory_space=pltpu.SMEM), vmem, vmem],
        out_specs=vmem,
        out_shape=pltpu.VMEM((n_clusters, half), jnp.float32),
        compiler_params=pltpu.CompilerParams(vmem_limit_bytes=8 * MIB),
        cost_estimate=pl.CostEstimate(
            flops=2 * n_clusters * n_docs * half, bytes_accessed=2 * n_docs * (n_clusters + half), transcendentals=0
        ),
        name="own",
    )(core, plan, documents)


def sum_kernel(got_ref, out_ref):
    total = sum_slots(got_ref).astype(out_ref.dtype)
    for slot in range(out_ref.shape[0]):
        out_ref[slot] = total


def sum_call(got, copies):
    vmem = pl.BlockSpec(memory_space=pltpu.VMEM)
    return pl.pallas_call(
        sum_kernel,
        in_specs=[vmem],
        out_specs=vmem,
        out_shape=pltpu.VMEM((copies, *got.shape[1:]), got.dtype),
        compiler_params=pltpu.CompilerParams(vmem_limit_bytes=4 * MIB),
        name="sum",
    )(got)


def pack_kernel(own_ref, got_ref, mass_ref, mass_got_ref, out_ref):
    n_slabs = out_ref.shape[0]
    slab = own_ref.shape[0] // n_slabs
    mass = mass_ref[0] + mass_got_ref[0]
    high = mass.astype(jnp.bfloat16)
    low = (mass - high.astype(jnp.float32)).astype(jnp.bfloat16)
    for k in range(n_slabs):
        rows = slice(k * slab, (k + 1) * slab)
        total = (own_ref[rows, :] + got_ref[rows, :].astype(jnp.float32)).astype(jnp.bfloat16)
        pieces = [total[:, lane : lane + LANES] for lane in range(0, own_ref.shape[1], LANES)] + [high, low]
        first = 0
        for piece in pieces:
            out_ref[k, first : first + piece.shape[0], :] = piece
            first += piece.shape[0]


def pack_call(own, got, mass, mass_got):
    n_clusters, half = own.shape
    n_slabs = NX * NY
    rows = n_clusters // n_slabs * (half // LANES) + 2 * mass.shape[1]
    vmem = pl.BlockSpec(memory_space=pltpu.VMEM)
    return pl.pallas_call(
        pack_kernel,
        in_specs=[vmem] * 4,
        out_specs=vmem,
        out_shape=pltpu.VMEM((n_slabs, rows, LANES), jnp.bfloat16),
        compiler_params=pltpu.CompilerParams(vmem_limit_bytes=8 * MIB),
        name="pack",
    )(own, got, mass, mass_got)


def repack_kernel(slab, got_ref, out_ref):
    groups = out_ref.shape[2] // LANES - 2
    rows = slab // NZ
    total = sum_slots(got_ref)
    mass = total[groups * slab : groups * slab + 8] + total[groups * slab + 8 :]
    high = mass.astype(jnp.bfloat16)
    low = (mass - high.astype(jnp.float32)).astype(jnp.bfloat16)
    total = total.astype(jnp.bfloat16)
    for k in range(NZ):
        for group in range(groups):
            first = group * slab + k * rows
            out_ref[k, :, group * LANES : (group + 1) * LANES] = total[first : first + rows]
        out_ref[k, :, groups * LANES : (groups + 1) * LANES] = high
        out_ref[k, :, (groups + 1) * LANES :] = low


def repack_call(got, slab):
    groups = (got.shape[1] - 16) // slab
    vmem = pl.BlockSpec(memory_space=pltpu.VMEM)
    return pl.pallas_call(
        functools.partial(repack_kernel, slab),
        in_specs=[vmem],
        out_specs=vmem,
        out_shape=pltpu.VMEM((NZ, slab // NZ, (groups + 2) * LANES), jnp.bfloat16),
        compiler_params=pltpu.CompilerParams(vmem_limit_bytes=8 * MIB),
        name="repack",
    )(got)


def finish_kernel(place_ref, got_ref, cluster_mass_ref, out_ref, duals_ref):
    total = sum_slots(got_ref)
    half = out_ref.shape[2]
    mass = total[:, half : half + LANES] + total[:, half + LANES :]
    duals_ref[...] = TAU * (jnp.log(cluster_mass_ref[...]) - jnp.log(mass))
    place = place_ref[0]
    group = place // LANES
    first = place - group * LANES
    row = lax.broadcasted_iota(jnp.int32, mass.shape, 0)
    lane = lax.broadcasted_iota(jnp.int32, mass.shape, 1)
    line = jnp.sum(jnp.where(row == group, mass, 0.0), axis=0, keepdims=True)
    mine = jnp.where(lane == row + first, jnp.broadcast_to(line, mass.shape), 0.0)
    own_mass = jnp.sum(mine, axis=1, keepdims=True)
    centroids = (total[:, :half] / own_mass).astype(jnp.bfloat16)
    for k in range(out_ref.shape[0]):
        out_ref[k] = centroids


def finish_call(got, cluster_mass, place):
    rows, half = got.shape[1], got.shape[2] - 2 * LANES
    vmem = pl.BlockSpec(memory_space=pltpu.VMEM)
    return pl.pallas_call(
        finish_kernel,
        in_specs=[pl.BlockSpec(memory_space=pltpu.SMEM), vmem, vmem],
        out_specs=[vmem, vmem],
        out_shape=[
            pltpu.VMEM((NX * NZ, rows, half), jnp.bfloat16),
            pltpu.VMEM(cluster_mass.shape, jnp.float32),
        ],
        compiler_params=pltpu.CompilerParams(vmem_limit_bytes=8 * MIB),
        name="finish",
    )(place, got, cluster_mass)


def write_kernel(core_ref, half_ref, *refs):
    out_hbm, sem = refs[-2:]
    half = half_ref.shape[1]
    columns = pl.ds(pl.multiple_of(core_ref[0] * half, half), half)
    copy = pltpu.make_async_copy(half_ref, out_hbm.at[:, columns], sem)
    copy.start()
    copy.wait()


def write_call(core, half, out):
    rows, width = half.shape
    hbm = pl.BlockSpec(memory_space=pltpu.HBM)
    specs = [pl.BlockSpec(memory_space=pltpu.SMEM), pl.BlockSpec(memory_space=pltpu.VMEM)]
    operands = (core, half) if out is None else (core, half, out)
    return pl.pallas_call(
        write_kernel,
        in_specs=specs + [hbm] * (len(operands) - 2),
        out_specs=hbm,
        out_shape=jax.ShapeDtypeStruct((rows, 2 * width), half.dtype),
        scratch_shapes=[pltpu.SemaphoreType.DMA],
        input_output_aliases={} if out is None else {2: 0},
        compiler_params=pltpu.CompilerParams(vmem_limit_bytes=4 * MIB),
        cost_estimate=pl.CostEstimate(flops=0, bytes_accessed=8 * rows * width, transcendentals=0),
        name="write",
    )(*operands)


def sum_all(copies):
    got = lax.all_to_all(copies, ("x", "y"), 0, 0, tiled=True)
    return lax.all_to_all(sum_call(got, NZ * NC), ("z", "c"), 0, 0, tiled=True)


def per_device(documents, centroids, cluster_mass):
    n_docs = documents.shape[0] * NX * NZ * NC * NY
    n_clusters = centroids.shape[0]
    half = documents.shape[1] // NC
    core = lax.axis_index("c")
    slab = n_clusters // (NX * NY)
    rows = slab // NZ
    place = (lax.axis_index("y") * NX + lax.axis_index("x")) * slab + lax.axis_index("z") * rows
    documents, core, place = lax.optimization_barrier((documents, core.reshape(1), place.reshape(1)))
    loga = -math.log2(n_docs)
    cluster_mass = cluster_mass.reshape(n_clusters // LANES, LANES)
    scores, mass, documents = first_call(documents, centroids, loga)
    mass = middle_call(scores, sum_all(mass), cluster_mass, loga)
    send, plan, mass = last_call(scores, sum_all(mass), cluster_mass, documents, core, loga)
    own = own_call(plan, documents, core)
    packed = pack_call(own, swap_cores(send), mass, swap_cores(mass))
    packed = repack_call(lax.all_to_all(packed, ("y", "x"), 0, 0, tiled=True), slab)
    packed = lax.all_to_all(packed, ("z",), 0, 0, tiled=True)
    mine, duals = finish_call(packed, cluster_mass, place)
    block = lax.all_to_all(mine, ("x", "z"), 0, 0, tiled=True).reshape(n_clusters // NY, half)
    other = swap_cores(block)
    out = write_call(core, block, None)
    return write_call(1 - core, other, out), duals.reshape(n_clusters)


def solution(mesh):
    grid = Mesh(mesh.devices.reshape(NX, NZ, NC, NY), AXES)
    return jax.shard_map(
        per_device,
        mesh=grid,
        in_specs=(P(AXES, None), P(), P()),
        out_specs=(P("y", None), P()),
        check_vma=False,
    )
```

```python
import functools
import math

import jax
import jax.numpy as jnp
from jax import lax
from jax.experimental import pallas as pl
from jax.experimental.pallas import tpu as pltpu
from jax.sharding import Mesh
from jax.sharding import PartitionSpec as P

D = 1024
TAU = 0.8
TEMP = 4.0
NX, NZ, NC, NY = 4, 8, 2, 4
AXES = ("x", "z", "c", "y")
LANES = 128
BLOCK = 512
CHUNK = 64
LOG2E = 1 / math.log(2)
MIB = 2**20


def swap_cores(value):
    return lax.ppermute(value, "c", [(0, 1), (1, 0)])


def fold(value, op):
    return op(value.reshape(value.shape[0] // 8, 8, value.shape[1]), axis=0)


def block_masses(scores_ref, columns, duals_ref, loga, emit):
    n_clusters = scores_ref.shape[0]
    width = columns.stop - columns.start

    def shifted(row):
        value = scores_ref[row : row + CHUNK, columns]
        if duals_ref is None:
            return value
        duals = duals_ref[row : row + CHUNK, :]
        return value + jnp.concatenate([duals] * (width // LANES), axis=1)

    top = fold(shifted(0), jnp.max)
    for row in range(CHUNK, n_clusters, CHUNK):
        top = jnp.maximum(top, fold(shifted(row), jnp.max))
    top = jnp.max(top, axis=0, keepdims=True)
    total = fold(jnp.exp2(shifted(0) - top), jnp.sum)
    for row in range(CHUNK, n_clusters, CHUNK):
        total += fold(jnp.exp2(shifted(row) - top), jnp.sum)
    lse = top + jnp.log2(jnp.sum(total, axis=0, keepdims=True))
    row_duals = TAU * (loga - lse)
    for row in range(0, n_clusters, CHUNK):
        emit(row, jnp.exp2(scores_ref[row : row + CHUNK, columns] + row_duals))


def add_lanes(acc, row, mass):
    total = mass[:, :LANES]
    for lane in range(LANES, mass.shape[1], LANES):
        total += mass[:, lane : lane + LANES]
    acc[row : row + CHUNK, :] += total


def column_sums(acc, out_ref):
    rows = [jnp.sum(acc[k : k + LANES, :].T, axis=0, keepdims=True) for k in range(0, acc.shape[0], LANES)]
    sums = jnp.concatenate(rows, axis=0).astype(out_ref.dtype)
    for slot in range(out_ref.shape[0]):
        out_ref[slot] = sums


def sum_slots(got_ref):
    total = got_ref[0].astype(jnp.float32)
    for slot in range(1, got_ref.shape[0]):
        total += got_ref[slot].astype(jnp.float32)
    return total


def start_duals(got_ref, cluster_mass_ref, duals_col):
    column_mass = sum_slots(got_ref)
    duals = TAU * (jnp.log2(cluster_mass_ref[...]) - jnp.log2(column_mass))
    for k in range(duals.shape[0]):
        row = jnp.broadcast_to(duals[k : k + 1, :], (LANES, LANES))
        duals_col[k * LANES : (k + 1) * LANES, :] = row.T


def first_kernel(loga, docs_hbm, cent_hbm, scores_ref, mass_ref, docs_ref, cent_ref, acc, sems):
    n_blocks = scores_ref.shape[0]
    copies = [pltpu.make_async_copy(cent_hbm, cent_ref, sems.at[n_blocks])]
    for block in range(n_blocks):
        rows = pl.ds(block * BLOCK, BLOCK)
        copies.append(pltpu.make_async_copy(docs_hbm.at[rows], docs_ref.at[rows], sems.at[block]))
    for copy in copies[:2]:
        copy.start()
    acc[...] = jnp.zeros_like(acc)
    copies[0].wait()
    start, ready = 0, []
    for group in (1, n_blocks - 1):
        blocks = range(start, start + group)
        for block in blocks:
            copies[block + 1].wait()
        if start == 0:
            for copy in copies[2:]:
                copy.start()
        scores = lax.dot_general(
            cent_ref[...],
            docs_ref[start * BLOCK : (start + group) * BLOCK, :],
            (((1,), (1,)), ((), ())),
            preferred_element_type=jnp.float32,
        ) * (TEMP / math.sqrt(D) * LOG2E)
        for k, block in enumerate(blocks):
            scores_ref[block] = scores[:, k * BLOCK : (k + 1) * BLOCK]
        for block in ready:
            block_masses(scores_ref.at[block], slice(0, BLOCK), None, loga, functools.partial(add_lanes, acc))
        start, ready = start + group, blocks
    for block in ready:
        block_masses(scores_ref.at[block], slice(0, BLOCK), None, loga, functools.partial(add_lanes, acc))
    column_sums(acc, mass_ref)


def first_call(documents, centroids, loga):
    n_docs, dim = documents.shape
    n_clusters = centroids.shape[0]
    n_blocks = n_docs // BLOCK
    vmem = pl.BlockSpec(memory_space=pltpu.VMEM)
    return pl.pallas_call(
        functools.partial(first_kernel, loga),
        in_specs=[pl.BlockSpec(memory_space=pltpu.HBM)] * 2,
        out_specs=[vmem] * 3,
        out_shape=[
            pltpu.VMEM((n_blocks, n_clusters, BLOCK), jnp.float32),
            pltpu.VMEM((NX * NY, n_clusters // LANES, LANES), jnp.bfloat16),
            pltpu.VMEM((n_docs, dim), jnp.bfloat16),
        ],
        scratch_shapes=[
            pltpu.VMEM((n_clusters, dim), jnp.bfloat16),
            pltpu.VMEM((n_clusters, LANES), jnp.float32),
            pltpu.SemaphoreType.DMA((n_blocks + 1,)),
        ],
        compiler_params=pltpu.CompilerParams(vmem_limit_bytes=50 * MIB),
        name="first",
    )(documents, centroids)


def middle_kernel(loga, scores_ref, got_ref, cluster_mass_ref, mass_ref, duals_col, acc):
    start_duals(got_ref, cluster_mass_ref, duals_col)
    acc[...] = jnp.zeros_like(acc)

    @pl.loop(0, scores_ref.shape[0])
    def _(block):
        block_masses(scores_ref.at[block], slice(0, BLOCK), duals_col, loga, functools.partial(add_lanes, acc))

    column_sums(acc, mass_ref)


def middle_call(scores, got, cluster_mass, loga):
    n_clusters = scores.shape[1]
    vmem = pl.BlockSpec(memory_space=pltpu.VMEM)
    return pl.pallas_call(
        functools.partial(middle_kernel, loga),
        in_specs=[vmem] * 3,
        out_specs=vmem,
        out_shape=pltpu.VMEM((NX * NY, n_clusters // LANES, LANES), jnp.bfloat16),
        scratch_shapes=[
            pltpu.VMEM((n_clusters, LANES), jnp.float32),
            pltpu.VMEM((n_clusters, LANES), jnp.float32),
        ],
        compiler_params=pltpu.CompilerParams(vmem_limit_bytes=8 * MIB),
        name="middle",
    )(scores, got, cluster_mass)


def half_columns(core, half):
    return pl.ds(pl.multiple_of(core * half, half), half)


def last_kernel(loga, core_ref, scores_ref, got_ref, cluster_mass_ref, docs_ref, send_ref, plan_ref, mass_ref, total, duals_col, acc):
    n_blocks = scores_ref.shape[0]
    columns = half_columns(1 - core_ref[0], send_ref.shape[1])
    start_duals(got_ref, cluster_mass_ref, duals_col)
    acc[...] = jnp.zeros_like(acc)
    for block in range(n_blocks + 1):
        if block > 0:
            rows = slice((block - 1) * BLOCK, block * BLOCK)
            part = lax.dot_general(
                plan_ref[:, rows], docs_ref[rows, columns], (((1,), (0,)), ((), ())), preferred_element_type=jnp.float32
            )
            if block > 1:
                part += total[...]
            if block < n_blocks:
                total[...] = part
            else:
                send_ref[...] = part.astype(jnp.bfloat16)
        if block < n_blocks:

            def emit(row, mass, start=block * BLOCK):
                add_lanes(acc, row, mass)
                plan_ref[row : row + CHUNK, start : start + BLOCK] = mass.astype(jnp.bfloat16)

            block_masses(scores_ref.at[block], slice(0, BLOCK), duals_col, loga, emit)
    column_sums(acc, mass_ref)


def last_call(scores, got, cluster_mass, documents, core, loga):
    n_clusters = scores.shape[1]
    n_docs, dim = documents.shape
    half = dim // NC
    vmem = pl.BlockSpec(memory_space=pltpu.VMEM)
    return pl.pallas_call(
        functools.partial(last_kernel, loga),
        in_specs=[pl.BlockSpec(memory_space=pltpu.SMEM)] + [vmem] * 4,
        out_specs=[vmem] * 3,
        out_shape=[
            pltpu.VMEM((n_clusters, half), jnp.bfloat16),
            pltpu.VMEM((n_clusters, n_docs), jnp.bfloat16),
            pltpu.VMEM((1, n_clusters // LANES, LANES), jnp.float32),
        ],
        scratch_shapes=[
            pltpu.VMEM((n_clusters, half), jnp.float32),
            pltpu.VMEM((n_clusters, LANES), jnp.float32),
            pltpu.VMEM((n_clusters, LANES), jnp.float32),
        ],
        compiler_params=pltpu.CompilerParams(vmem_limit_bytes=16 * MIB),
        name="last",
    )(core, scores, got, cluster_mass, documents)


def own_kernel(core_ref, plan_ref, docs_ref, own_ref):
    half = own_ref.shape[1]
    own_ref[...] = lax.dot_general(
        plan_ref[...],
        docs_ref[:, half_columns(core_ref[0], half)],
        (((1,), (0,)), ((), ())),
        preferred_element_type=jnp.float32,
    )


def own_call(plan, documents, core):
    n_clusters, n_docs = plan.shape
    half = documents.shape[1] // NC
    vmem = pl.BlockSpec(memory_space=pltpu.VMEM)
    return pl.pallas_call(
        own_kernel,
        in_specs=[pl.BlockSpec(memory_space=pltpu.SMEM), vmem, vmem],
        out_specs=vmem,
        out_shape=pltpu.VMEM((n_clusters, half), jnp.float32),
        compiler_params=pltpu.CompilerParams(vmem_limit_bytes=8 * MIB),
        cost_estimate=pl.CostEstimate(
            flops=2 * n_clusters * n_docs * half, bytes_accessed=2 * n_docs * (n_clusters + half), transcendentals=0
        ),
        name="own",
    )(core, plan, documents)


def sum_kernel(got_ref, out_ref):
    total = sum_slots(got_ref).astype(out_ref.dtype)
    for slot in range(out_ref.shape[0]):
        out_ref[slot] = total


def sum_call(got, copies):
    vmem = pl.BlockSpec(memory_space=pltpu.VMEM)
    return pl.pallas_call(
        sum_kernel,
        in_specs=[vmem],
        out_specs=vmem,
        out_shape=pltpu.VMEM((copies, *got.shape[1:]), got.dtype),
        compiler_params=pltpu.CompilerParams(vmem_limit_bytes=4 * MIB),
        name="sum",
    )(got)


def pack_kernel(own_ref, got_ref, mass_ref, mass_got_ref, out_ref):
    n_slabs = out_ref.shape[0]
    slab = own_ref.shape[0] // n_slabs
    mass = mass_ref[0] + mass_got_ref[0]
    high = mass.astype(jnp.bfloat16)
    low = (mass - high.astype(jnp.float32)).astype(jnp.bfloat16)
    for k in range(n_slabs):
        rows = slice(k * slab, (k + 1) * slab)
        total = (own_ref[rows, :] + got_ref[rows, :].astype(jnp.float32)).astype(jnp.bfloat16)
        pieces = [total[:, lane : lane + LANES] for lane in range(0, own_ref.shape[1], LANES)] + [high, low]
        first = 0
        for piece in pieces:
            out_ref[k, first : first + piece.shape[0], :] = piece
            first += piece.shape[0]


def pack_call(own, got, mass, mass_got):
    n_clusters, half = own.shape
    n_slabs = NX * NY
    rows = n_clusters // n_slabs * (half // LANES) + 2 * mass.shape[1]
    vmem = pl.BlockSpec(memory_space=pltpu.VMEM)
    return pl.pallas_call(
        pack_kernel,
        in_specs=[vmem] * 4,
        out_specs=vmem,
        out_shape=pltpu.VMEM((n_slabs, rows, LANES), jnp.bfloat16),
        compiler_params=pltpu.CompilerParams(vmem_limit_bytes=8 * MIB),
        name="pack",
    )(own, got, mass, mass_got)


def repack_kernel(slab, got_ref, out_ref):
    groups = out_ref.shape[2] // LANES - 2
    rows = slab // NZ
    total = sum_slots(got_ref)
    mass = total[groups * slab : groups * slab + 8] + total[groups * slab + 8 :]
    high = mass.astype(jnp.bfloat16)
    low = (mass - high.astype(jnp.float32)).astype(jnp.bfloat16)
    total = total.astype(jnp.bfloat16)
    for k in range(NZ):
        for group in range(groups):
            first = group * slab + k * rows
            out_ref[k, :, group * LANES : (group + 1) * LANES] = total[first : first + rows]
        out_ref[k, :, groups * LANES : (groups + 1) * LANES] = high
        out_ref[k, :, (groups + 1) * LANES :] = low


def repack_call(got, slab):
    groups = (got.shape[1] - 16) // slab
    vmem = pl.BlockSpec(memory_space=pltpu.VMEM)
    return pl.pallas_call(
        functools.partial(repack_kernel, slab),
        in_specs=[vmem],
        out_specs=vmem,
        out_shape=pltpu.VMEM((NZ, slab // NZ, (groups + 2) * LANES), jnp.bfloat16),
        compiler_params=pltpu.CompilerParams(vmem_limit_bytes=8 * MIB),
        name="repack",
    )(got)


def finish_kernel(place_ref, got_ref, cluster_mass_ref, out_ref, duals_ref):
    total = sum_slots(got_ref)
    half = out_ref.shape[2]
    mass = total[:, half : half + LANES] + total[:, half + LANES :]
    duals_ref[...] = TAU * (jnp.log(cluster_mass_ref[...]) - jnp.log(mass))
    place = place_ref[0]
    group = place // LANES
    first = place - group * LANES
    row = lax.broadcasted_iota(jnp.int32, mass.shape, 0)
    lane = lax.broadcasted_iota(jnp.int32, mass.shape, 1)
    line = jnp.sum(jnp.where(row == group, mass, 0.0), axis=0, keepdims=True)
    mine = jnp.where(lane == row + first, jnp.broadcast_to(line, mass.shape), 0.0)
    own_mass = jnp.sum(mine, axis=1, keepdims=True)
    centroids = (total[:, :half] / own_mass).astype(jnp.bfloat16)
    for k in range(out_ref.shape[0]):
        out_ref[k] = centroids


def finish_call(got, cluster_mass, place):
    rows, half = got.shape[1], got.shape[2] - 2 * LANES
    vmem = pl.BlockSpec(memory_space=pltpu.VMEM)
    return pl.pallas_call(
        finish_kernel,
        in_specs=[pl.BlockSpec(memory_space=pltpu.SMEM), vmem, vmem],
        out_specs=[vmem, vmem],
        out_shape=[
            pltpu.VMEM((NX * NZ, rows, half), jnp.bfloat16),
            pltpu.VMEM(cluster_mass.shape, jnp.float32),
        ],
        compiler_params=pltpu.CompilerParams(vmem_limit_bytes=8 * MIB),
        name="finish",
    )(place, got, cluster_mass)


def write_kernel(core_ref, half_ref, *refs):
    out_hbm, sem = refs[-2:]
    half = half_ref.shape[1]
    columns = pl.ds(pl.multiple_of(core_ref[0] * half, half), half)
    copy = pltpu.make_async_copy(half_ref, out_hbm.at[:, columns], sem)
    copy.start()
    copy.wait()


def write_call(core, half, out):
    rows, width = half.shape
    hbm = pl.BlockSpec(memory_space=pltpu.HBM)
    specs = [pl.BlockSpec(memory_space=pltpu.SMEM), pl.BlockSpec(memory_space=pltpu.VMEM)]
    operands = (core, half) if out is None else (core, half, out)
    return pl.pallas_call(
        write_kernel,
        in_specs=specs + [hbm] * (len(operands) - 2),
        out_specs=hbm,
        out_shape=jax.ShapeDtypeStruct((rows, 2 * width), half.dtype),
        scratch_shapes=[pltpu.SemaphoreType.DMA],
        input_output_aliases={} if out is None else {2: 0},
        compiler_params=pltpu.CompilerParams(vmem_limit_bytes=4 * MIB),
        cost_estimate=pl.CostEstimate(flops=0, bytes_accessed=8 * rows * width, transcendentals=0),
        name="write",
    )(*operands)


def sum_all(copies):
    got = lax.all_to_all(copies, ("x", "y"), 0, 0, tiled=True)
    return lax.all_to_all(sum_call(got, NZ * NC), ("z", "c"), 0, 0, tiled=True)


def per_device(documents, centroids, cluster_mass):
    n_docs = documents.shape[0] * NX * NZ * NC * NY
    n_clusters = centroids.shape[0]
    half = documents.shape[1] // NC
    core = lax.axis_index("c")
    slab = n_clusters // (NX * NY)
    rows = slab // NZ
    place = (lax.axis_index("y") * NX + lax.axis_index("x")) * slab + lax.axis_index("z") * rows
    documents, core, place = lax.optimization_barrier((documents, core.reshape(1), place.reshape(1)))
    loga = -math.log2(n_docs)
    cluster_mass = cluster_mass.reshape(n_clusters // LANES, LANES)
    scores, mass, documents = first_call(documents, centroids, loga)
    mass = middle_call(scores, sum_all(mass), cluster_mass, loga)
    send, plan, mass = last_call(scores, sum_all(mass), cluster_mass, documents, core, loga)
    own = own_call(plan, documents, core)
    packed = pack_call(own, swap_cores(send), mass, swap_cores(mass))
    packed = repack_call(lax.all_to_all(packed, ("y", "x"), 0, 0, tiled=True), slab)
    packed = lax.all_to_all(packed, ("z",), 0, 0, tiled=True)
    mine, duals = finish_call(packed, cluster_mass, place)
    block = lax.all_to_all(mine, ("x", "z"), 0, 0, tiled=True).reshape(n_clusters // NY, half)
    other = swap_cores(block)
    out = write_call(core, block, None)
    return write_call(1 - core, other, out), duals.reshape(n_clusters)


def solution(mesh):
    grid = Mesh(mesh.devices.reshape(NX, NZ, NC, NY), AXES)
    return jax.shard_map(
        per_device,
        mesh=grid,
        in_specs=(P(AXES, None), P(), P()),
        out_specs=(P("y", None), P()),
        check_vma=False,
    )
```

```python
import functools
import math

import jax
import jax.numpy as jnp
from jax import lax
from jax.experimental import pallas as pl
from jax.experimental.pallas import tpu as pltpu
from jax.sharding import Mesh
from jax.sharding import PartitionSpec as P

D = 1024
TAU = 0.8
TEMP = 4.0
NX, NZ, NC, NY = 4, 8, 2, 4
AXES = ("x", "z", "c", "y")
LANES = 128
BLOCK = 512
GROUP = 2
CHUNK = 64
LOG2E = 1 / math.log(2)
MIB = 2**20


def swap_cores(value):
    return lax.ppermute(value, "c", [(0, 1), (1, 0)])


def fold(value, op):
    return op(value.reshape(value.shape[0] // 8, 8, value.shape[1]), axis=0)


def block_masses(scores_ref, columns, duals_ref, loga, emit):
    n_clusters = scores_ref.shape[0]
    width = columns.stop - columns.start

    def shifted(row):
        value = scores_ref[row : row + CHUNK, columns]
        if duals_ref is None:
            return value
        duals = duals_ref[row : row + CHUNK, :]
        return value + jnp.concatenate([duals] * (width // LANES), axis=1)

    top = fold(shifted(0), jnp.max)
    for row in range(CHUNK, n_clusters, CHUNK):
        top = jnp.maximum(top, fold(shifted(row), jnp.max))
    top = jnp.max(top, axis=0, keepdims=True)
    total = fold(jnp.exp2(shifted(0) - top), jnp.sum)
    for row in range(CHUNK, n_clusters, CHUNK):
        total += fold(jnp.exp2(shifted(row) - top), jnp.sum)
    lse = top + jnp.log2(jnp.sum(total, axis=0, keepdims=True))
    row_duals = TAU * (loga - lse)
    for row in range(0, n_clusters, CHUNK):
        emit(row, jnp.exp2(scores_ref[row : row + CHUNK, columns] + row_duals))


def add_lanes(acc, row, mass):
    total = mass[:, :LANES]
    for lane in range(LANES, mass.shape[1], LANES):
        total += mass[:, lane : lane + LANES]
    acc[row : row + CHUNK, :] += total


def column_sums(acc, out_ref):
    rows = [jnp.sum(acc[k : k + LANES, :].T, axis=0, keepdims=True) for k in range(0, acc.shape[0], LANES)]
    sums = jnp.concatenate(rows, axis=0).astype(out_ref.dtype)
    for slot in range(out_ref.shape[0]):
        out_ref[slot] = sums


def sum_slots(got_ref):
    total = got_ref[0].astype(jnp.float32)
    for slot in range(1, got_ref.shape[0]):
        total += got_ref[slot].astype(jnp.float32)
    return total


def start_duals(got_ref, cluster_mass_ref, duals_col):
    column_mass = sum_slots(got_ref)
    duals = TAU * (jnp.log2(cluster_mass_ref[...]) - jnp.log2(column_mass))
    for k in range(duals.shape[0]):
        row = jnp.broadcast_to(duals[k : k + 1, :], (LANES, LANES))
        duals_col[k * LANES : (k + 1) * LANES, :] = row.T


def first_kernel(loga, docs_hbm, cent_hbm, scores_ref, mass_ref, docs_ref, cent_ref, acc, sems):
    n_blocks = scores_ref.shape[0]
    copies = [pltpu.make_async_copy(cent_hbm, cent_ref, sems.at[n_blocks])]
    for block in range(n_blocks):
        rows = pl.ds(block * BLOCK, BLOCK)
        copies.append(pltpu.make_async_copy(docs_hbm.at[rows], docs_ref.at[rows], sems.at[block]))
    for copy in copies[: 1 + GROUP]:
        copy.start()
    acc[...] = jnp.zeros_like(acc)
    copies[0].wait()
    for block in range(n_blocks + 1):
        if block % GROUP == 0 and block < n_blocks:
            for k in range(block, block + GROUP):
                copies[k + 1].wait()
            if block == 0:
                for copy in copies[1 + GROUP :]:
                    copy.start()
            scores = lax.dot_general(
                cent_ref[...],
                docs_ref[block * BLOCK : (block + GROUP) * BLOCK, :],
                (((1,), (1,)), ((), ())),
                preferred_element_type=jnp.float32,
            ) * (TEMP / math.sqrt(D) * LOG2E)
            for k in range(GROUP):
                scores_ref[block + k] = scores[:, k * BLOCK : (k + 1) * BLOCK]
        if block > 0:
            block_masses(scores_ref.at[block - 1], slice(0, BLOCK), None, loga, functools.partial(add_lanes, acc))
    column_sums(acc, mass_ref)


def first_call(documents, centroids, loga):
    n_docs, dim = documents.shape
    n_clusters = centroids.shape[0]
    n_blocks = n_docs // BLOCK
    vmem = pl.BlockSpec(memory_space=pltpu.VMEM)
    return pl.pallas_call(
        functools.partial(first_kernel, loga),
        in_specs=[pl.BlockSpec(memory_space=pltpu.HBM)] * 2,
        out_specs=[vmem] * 3,
        out_shape=[
            pltpu.VMEM((n_blocks, n_clusters, BLOCK), jnp.float32),
            pltpu.VMEM((NZ * NC, n_clusters // LANES, LANES), jnp.bfloat16),
            pltpu.VMEM((n_docs, dim), jnp.bfloat16),
        ],
        scratch_shapes=[
            pltpu.VMEM((n_clusters, dim), jnp.bfloat16),
            pltpu.VMEM((n_clusters, LANES), jnp.float32),
            pltpu.SemaphoreType.DMA((n_blocks + 1,)),
        ],
        compiler_params=pltpu.CompilerParams(vmem_limit_bytes=50 * MIB),
        name="first",
    )(documents, centroids)


def middle_kernel(loga, scores_ref, got_ref, cluster_mass_ref, mass_ref, duals_col, acc):
    start_duals(got_ref, cluster_mass_ref, duals_col)
    acc[...] = jnp.zeros_like(acc)

    @pl.loop(0, scores_ref.shape[0])
    def _(block):
        block_masses(scores_ref.at[block], slice(0, BLOCK), duals_col, loga, functools.partial(add_lanes, acc))

    column_sums(acc, mass_ref)


def middle_call(scores, got, cluster_mass, loga):
    n_clusters = scores.shape[1]
    vmem = pl.BlockSpec(memory_space=pltpu.VMEM)
    return pl.pallas_call(
        functools.partial(middle_kernel, loga),
        in_specs=[vmem] * 3,
        out_specs=vmem,
        out_shape=pltpu.VMEM((NZ * NC, n_clusters // LANES, LANES), jnp.bfloat16),
        scratch_shapes=[
            pltpu.VMEM((n_clusters, LANES), jnp.float32),
            pltpu.VMEM((n_clusters, LANES), jnp.float32),
        ],
        compiler_params=pltpu.CompilerParams(vmem_limit_bytes=8 * MIB),
        name="middle",
    )(scores, got, cluster_mass)


def half_columns(core, half):
    return pl.ds(pl.multiple_of(core * half, half), half)


def last_kernel(loga, core_ref, scores_ref, got_ref, cluster_mass_ref, docs_ref, send_ref, plan_ref, mass_ref, total, duals_col, acc):
    n_blocks = scores_ref.shape[0]
    columns = half_columns(1 - core_ref[0], send_ref.shape[1])
    start_duals(got_ref, cluster_mass_ref, duals_col)
    acc[...] = jnp.zeros_like(acc)
    for block in range(n_blocks + 1):
        if block > 0:
            rows = slice((block - 1) * BLOCK, block * BLOCK)
            part = lax.dot_general(
                plan_ref[:, rows], docs_ref[rows, columns], (((1,), (0,)), ((), ())), preferred_element_type=jnp.float32
            )
            if block > 1:
                part += total[...]
            if block < n_blocks:
                total[...] = part
            else:
                send_ref[...] = part.astype(jnp.bfloat16)
        if block < n_blocks:

            def emit(row, mass, start=block * BLOCK):
                add_lanes(acc, row, mass)
                plan_ref[row : row + CHUNK, start : start + BLOCK] = mass.astype(jnp.bfloat16)

            block_masses(scores_ref.at[block], slice(0, BLOCK), duals_col, loga, emit)
    column_sums(acc, mass_ref)


def last_call(scores, got, cluster_mass, documents, core, loga):
    n_clusters = scores.shape[1]
    n_docs, dim = documents.shape
    half = dim // NC
    vmem = pl.BlockSpec(memory_space=pltpu.VMEM)
    return pl.pallas_call(
        functools.partial(last_kernel, loga),
        in_specs=[pl.BlockSpec(memory_space=pltpu.SMEM)] + [vmem] * 4,
        out_specs=[vmem] * 3,
        out_shape=[
            pltpu.VMEM((n_clusters, half), jnp.bfloat16),
            pltpu.VMEM((n_clusters, n_docs), jnp.bfloat16),
            pltpu.VMEM((1, n_clusters // LANES, LANES), jnp.float32),
        ],
        scratch_shapes=[
            pltpu.VMEM((n_clusters, half), jnp.float32),
            pltpu.VMEM((n_clusters, LANES), jnp.float32),
            pltpu.VMEM((n_clusters, LANES), jnp.float32),
        ],
        compiler_params=pltpu.CompilerParams(vmem_limit_bytes=16 * MIB),
        name="last",
    )(core, scores, got, cluster_mass, documents)


def own_kernel(core_ref, plan_ref, docs_ref, own_ref):
    half = own_ref.shape[1]
    own_ref[...] = lax.dot_general(
        plan_ref[...],
        docs_ref[:, half_columns(core_ref[0], half)],
        (((1,), (0,)), ((), ())),
        preferred_element_type=jnp.float32,
    )


def own_call(plan, documents, core):
    n_clusters, n_docs = plan.shape
    half = documents.shape[1] // NC
    vmem = pl.BlockSpec(memory_space=pltpu.VMEM)
    return pl.pallas_call(
        own_kernel,
        in_specs=[pl.BlockSpec(memory_space=pltpu.SMEM), vmem, vmem],
        out_specs=vmem,
        out_shape=pltpu.VMEM((n_clusters, half), jnp.float32),
        compiler_params=pltpu.CompilerParams(vmem_limit_bytes=8 * MIB),
        cost_estimate=pl.CostEstimate(
            flops=2 * n_clusters * n_docs * half, bytes_accessed=2 * n_docs * (n_clusters + half), transcendentals=0
        ),
        name="own",
    )(core, plan, documents)


def sum_kernel(got_ref, out_ref):
    total = sum_slots(got_ref).astype(out_ref.dtype)
    for slot in range(out_ref.shape[0]):
        out_ref[slot] = total


def sum_call(got, copies):
    vmem = pl.BlockSpec(memory_space=pltpu.VMEM)
    return pl.pallas_call(
        sum_kernel,
        in_specs=[vmem],
        out_specs=vmem,
        out_shape=pltpu.VMEM((copies, *got.shape[1:]), got.dtype),
        compiler_params=pltpu.CompilerParams(vmem_limit_bytes=4 * MIB),
        name="sum",
    )(got)


def pack_kernel(own_ref, got_ref, mass_ref, mass_got_ref, out_ref):
    n_slabs = out_ref.shape[0]
    slab = own_ref.shape[0] // n_slabs
    mass = mass_ref[0] + mass_got_ref[0]
    high = mass.astype(jnp.bfloat16)
    low = (mass - high.astype(jnp.float32)).astype(jnp.bfloat16)
    for k in range(n_slabs):
        rows = slice(k * slab, (k + 1) * slab)
        total = (own_ref[rows, :] + got_ref[rows, :].astype(jnp.float32)).astype(jnp.bfloat16)
        pieces = [total[:, lane : lane + LANES] for lane in range(0, own_ref.shape[1], LANES)] + [high, low]
        first = 0
        for piece in pieces:
            out_ref[k, first : first + piece.shape[0], :] = piece
            first += piece.shape[0]


def pack_call(own, got, mass, mass_got):
    n_clusters, half = own.shape
    n_slabs = NX * NY
    rows = n_clusters // n_slabs * (half // LANES) + 2 * mass.shape[1]
    vmem = pl.BlockSpec(memory_space=pltpu.VMEM)
    return pl.pallas_call(
        pack_kernel,
        in_specs=[vmem] * 4,
        out_specs=vmem,
        out_shape=pltpu.VMEM((n_slabs, rows, LANES), jnp.bfloat16),
        compiler_params=pltpu.CompilerParams(vmem_limit_bytes=8 * MIB),
        name="pack",
    )(own, got, mass, mass_got)


def repack_kernel(slab, got_ref, out_ref):
    groups = out_ref.shape[2] // LANES - 2
    rows = slab // NZ
    total = sum_slots(got_ref)
    mass = total[groups * slab : groups * slab + 8] + total[groups * slab + 8 :]
    high = mass.astype(jnp.bfloat16)
    low = (mass - high.astype(jnp.float32)).astype(jnp.bfloat16)
    total = total.astype(jnp.bfloat16)
    for k in range(NZ):
        for group in range(groups):
            first = group * slab + k * rows
            out_ref[k, :, group * LANES : (group + 1) * LANES] = total[first : first + rows]
        out_ref[k, :, groups * LANES : (groups + 1) * LANES] = high
        out_ref[k, :, (groups + 1) * LANES :] = low


def repack_call(got, slab):
    groups = (got.shape[1] - 16) // slab
    vmem = pl.BlockSpec(memory_space=pltpu.VMEM)
    return pl.pallas_call(
        functools.partial(repack_kernel, slab),
        in_specs=[vmem],
        out_specs=vmem,
        out_shape=pltpu.VMEM((NZ, slab // NZ, (groups + 2) * LANES), jnp.bfloat16),
        compiler_params=pltpu.CompilerParams(vmem_limit_bytes=8 * MIB),
        name="repack",
    )(got)


def finish_kernel(place_ref, got_ref, cluster_mass_ref, out_ref, duals_ref):
    total = sum_slots(got_ref)
    half = out_ref.shape[2]
    mass = total[:, half : half + LANES] + total[:, half + LANES :]
    duals_ref[...] = TAU * (jnp.log(cluster_mass_ref[...]) - jnp.log(mass))
    place = place_ref[0]
    group = place // LANES
    first = place - group * LANES
    row = lax.broadcasted_iota(jnp.int32, mass.shape, 0)
    lane = lax.broadcasted_iota(jnp.int32, mass.shape, 1)
    line = jnp.sum(jnp.where(row == group, mass, 0.0), axis=0, keepdims=True)
    mine = jnp.where(lane == row + first, jnp.broadcast_to(line, mass.shape), 0.0)
    own_mass = jnp.sum(mine, axis=1, keepdims=True)
    centroids = (total[:, :half] / own_mass).astype(jnp.bfloat16)
    for k in range(out_ref.shape[0]):
        out_ref[k] = centroids


def finish_call(got, cluster_mass, place):
    rows, half = got.shape[1], got.shape[2] - 2 * LANES
    vmem = pl.BlockSpec(memory_space=pltpu.VMEM)
    return pl.pallas_call(
        finish_kernel,
        in_specs=[pl.BlockSpec(memory_space=pltpu.SMEM), vmem, vmem],
        out_specs=[vmem, vmem],
        out_shape=[
            pltpu.VMEM((NX * NZ, rows, half), jnp.bfloat16),
            pltpu.VMEM(cluster_mass.shape, jnp.float32),
        ],
        compiler_params=pltpu.CompilerParams(vmem_limit_bytes=8 * MIB),
        name="finish",
    )(place, got, cluster_mass)


def write_kernel(core_ref, half_ref, *refs):
    out_hbm, sem = refs[-2:]
    half = half_ref.shape[1]
    columns = pl.ds(pl.multiple_of(core_ref[0] * half, half), half)
    copy = pltpu.make_async_copy(half_ref, out_hbm.at[:, columns], sem)
    copy.start()
    copy.wait()


def write_call(core, half, out):
    rows, width = half.shape
    hbm = pl.BlockSpec(memory_space=pltpu.HBM)
    specs = [pl.BlockSpec(memory_space=pltpu.SMEM), pl.BlockSpec(memory_space=pltpu.VMEM)]
    operands = (core, half) if out is None else (core, half, out)
    return pl.pallas_call(
        write_kernel,
        in_specs=specs + [hbm] * (len(operands) - 2),
        out_specs=hbm,
        out_shape=jax.ShapeDtypeStruct((rows, 2 * width), half.dtype),
        scratch_shapes=[pltpu.SemaphoreType.DMA],
        input_output_aliases={} if out is None else {2: 0},
        compiler_params=pltpu.CompilerParams(vmem_limit_bytes=4 * MIB),
        cost_estimate=pl.CostEstimate(flops=0, bytes_accessed=8 * rows * width, transcendentals=0),
        name="write",
    )(*operands)


def sum_all(copies):
    got = lax.all_to_all(copies, ("z", "c"), 0, 0, tiled=True)
    return lax.all_to_all(sum_call(got, NX * NY), ("x", "y"), 0, 0, tiled=True)


def per_device(documents, centroids, cluster_mass):
    n_docs = documents.shape[0] * NX * NZ * NC * NY
    n_clusters = centroids.shape[0]
    half = documents.shape[1] // NC
    core = lax.axis_index("c")
    slab = n_clusters // (NX * NY)
    rows = slab // NZ
    place = (lax.axis_index("y") * NX + lax.axis_index("x")) * slab + lax.axis_index("z") * rows
    documents, core, place = lax.optimization_barrier((documents, core.reshape(1), place.reshape(1)))
    loga = -math.log2(n_docs)
    cluster_mass = cluster_mass.reshape(n_clusters // LANES, LANES)
    scores, mass, documents = first_call(documents, centroids, loga)
    mass = middle_call(scores, sum_all(mass), cluster_mass, loga)
    send, plan, mass = last_call(scores, sum_all(mass), cluster_mass, documents, core, loga)
    own = own_call(plan, documents, core)
    packed = pack_call(own, swap_cores(send), mass, swap_cores(mass))
    packed = repack_call(lax.all_to_all(packed, ("y", "x"), 0, 0, tiled=True), slab)
    packed = lax.all_to_all(packed, ("z",), 0, 0, tiled=True)
    mine, duals = finish_call(packed, cluster_mass, place)
    block = lax.all_to_all(mine, ("x", "z"), 0, 0, tiled=True).reshape(n_clusters // NY, half)
    other = swap_cores(block)
    out = write_call(core, block, None)
    return write_call(1 - core, other, out), duals.reshape(n_clusters)


def solution(mesh):
    grid = Mesh(mesh.devices.reshape(NX, NZ, NC, NY), AXES)
    return jax.shard_map(
        per_device,
        mesh=grid,
        in_specs=(P(AXES, None), P(), P()),
        out_specs=(P("y", None), P()),
        check_vma=False,
    )
```
